128 devices in a mesh: tok: 4 (over x), con: 2 (over y_hi), out: 16 (over y_lo, z, core).
Axes of the slice: x: 4, y: 4 (y_hi: 2, y_lo: 2; y = y_hi * 2 + y_lo), z: 4, core: 2. Of those that a mesh axis runs over, the one named last changes fastest.
Arguments:
- tokens: bfloat16 [2048, 10240], P('tok', ('con', 'out')), may hold values from -200 to 200, as said below
- gain: bfloat16 [10240], P(('con', 'out')), may hold values from 0.099609375 to 1.8984375
- up_weight: bfloat16 [10240, 2, 10240], P('con', None, 'out'), may hold values from -0.0625 to 0.0625
- down_weight: bfloat16 [20480, 10240], P(('con', 'out')), may hold values from -0.078125 to 0.078125
Outputs:
- block_out: bfloat16 [2048, 10240], P('tok', ('con', 'out'))
The draws below stay inside these ranges and needn't reach their ends.
Inputs may be any that keep to these rules, and one draw needn't show every extreme that they name: `tokens`: activations of the residual stream.
All inputs are finite; a program needn't handle non-finite values.
Results may differ from the reference program's by a relative error of at most 0.028.
Values may be sent and summed in bfloat16 or wider, within the bound.
A program may use at most 128 MiB of HBM per device.

```python
import jax
import jax.numpy as jnp
from jax import lax

D = 10240
FFW = 20480
TOKENS = 2048
UNITS = 640
N_CON = 2
N_OUT = 16


def draw_tokens(key, part):
    first, second, third = jax.random.split(key, 3)
    place = jnp.arange(D, dtype=jnp.float32) / D
    column_scale = jnp.power(10.0, 0.5 * place + 0.5 * jax.random.uniform(second, (D,), jnp.float32))
    base = jnp.clip(jax.random.normal(first, (TOKENS, D), jnp.float32), -5.0, 5.0)
    row_scale = jnp.power(10.0, jax.random.uniform(third, (TOKENS, 1), jnp.float32))
    return (0.3 * base * column_scale * row_scale).astype(jnp.bfloat16)


def raised(values, own_key, source, target, parts, factor):
    owner, partner = [(jnp.arange(values.shape[position]) // (values.shape[position] // parts)).reshape([-1 if axis == position else 1 for axis in range(values.ndim)]) for position in (source, target)]
    chosen = jax.random.permutation(own_key, parts)[partner]
    strong = (owner == chosen) | (owner == (partner + parts // 2) % parts)
    return jnp.where(strong, factor * values, values)


def shard_levels(rng, shape, cuts, least, top_value):
    def one(axis_at, shards_of):
        steps = jax.random.uniform(jax.random.fold_in(jax.random.fold_in(rng, 6), axis_at), (shards_of,), jnp.float32, least / len(cuts), top_value / len(cuts))
        return jnp.repeat(jnp.exp(steps), shape[axis_at] // shards_of).reshape((-1,) + (1,) * (len(shape) - axis_at - 1))

    level = one(*cuts[0])
    for cut in cuts[1:]:
        level = level * one(*cut)
    return level


def bell_draw(own_key, extent, scale, most, pieces=(), held_as=jnp.bfloat16):
    drawn = jax.random.normal(own_key, extent, jnp.float32) * scale
    if len(pieces) > 0:
        drawn = shard_levels(own_key, extent, pieces, -0.22, 0.18) * drawn
    return jnp.clip(drawn, min=-most, max=most).astype(held_as)


def bell_draw_with(key, extent, width, limit, cuts, heavy, kind=jnp.bfloat16):
    result = width * jax.random.normal(key, extent, jnp.float32)
    if cuts:
        result = result * shard_levels(key, extent, cuts, -0.22, 0.18)
    return jnp.clip(raised(result, jax.random.fold_in(key, 3), *heavy), -limit, limit).astype(kind)


def setup_inputs(seed: int = 0) -> dict:
    key_of = jax.random.split(jax.random.key(seed), 5)
    return {
        "tokens": draw_tokens(jax.random.fold_in(key_of[4], 71), 0),
        "gain": jnp.clip(1.0 + 0.18 * jax.random.normal(key_of[1], (D,), jnp.float32), 0.099609375, 1.8984375).astype(jnp.bfloat16),
        "up_weight": bell_draw(key_of[2], (D, N_CON, FFW // N_CON), D ** -0.5, 0.0625, ((0, 2), (2, 16))),
        "down_weight": bell_draw_with(key_of[3], (FFW, D), FFW ** -0.5, 0.078125, ((0, 32),), (0, 1, 32, 2.75)),
    }


def reference(tokens, gain, up_weight, down_weight):
    values = tokens.astype(jnp.float32)
    average = lax.optimization_barrier(jnp.sum(values, axis=1, keepdims=True)) / D
    variance = lax.optimization_barrier(jnp.sum(values * values, axis=1, keepdims=True)) / D - average * average
    normed = ((values - average) * lax.rsqrt(variance + 1e-05) * gain.astype(jnp.float32)).astype(jnp.bfloat16)
    up_matrix = up_weight.reshape(D, FFW)
    preact = jnp.dot(normed, up_matrix, preferred_element_type=jnp.float32)
    hidden = jax.nn.gelu(preact, approximate=False).astype(jnp.bfloat16)
    groups = N_CON * N_OUT

    def add_group(index, total):
        begin = (index * UNITS).astype(jnp.int32)
        hidden_part = lax.dynamic_slice_in_dim(hidden, begin, UNITS, 1)
        weight_part = lax.dynamic_slice_in_dim(down_weight, begin, UNITS, 0)
        term = jnp.dot(hidden_part, weight_part, preferred_element_type=jnp.float32).astype(jnp.bfloat16)
        term = lax.optimization_barrier(term)
        return total + term.astype(jnp.float32)
    start_total = jnp.zeros((TOKENS, D), jnp.float32)
    total = lax.fori_loop(jnp.int32(0), jnp.int32(groups), add_group, start_total)
    return total.astype(jnp.bfloat16)
```

```python
import functools

import jax
import jax.numpy as jnp
from jax import lax
from jax.experimental import pallas as pl
from jax.experimental.pallas import tpu as pltpu
from jax.sharding import PartitionSpec as P

D = 10240
RING = 4
MESH = pl.DeviceIdType.MESH
F32, BF16 = jnp.float32, jnp.bfloat16


def normalize(values, totals, gain_row):
    average = totals[0][:, None] / D
    variance = totals[1][:, None] / D - average * average
    return ((values - average) * lax.rsqrt(variance + 1e-05) * gain_row.astype(F32)).astype(BF16)


def place():
    con, out = lax.axis_index("con"), lax.axis_index("out")
    return con * 2 + out // 8, (out // 2) % RING, out % 2


def device(y, z, core):
    return (lax.axis_index("tok"), y // 2, (y % 2) * 8 + z * 2 + core)


def shifted(y, z, role, first, second):
    return (
        (y + first * role + second * (1 - role)) % RING,
        (z + first * (1 - role) + second * role) % RING,
    )


def offset(j):
    swapped = j + (j // 2) * (5 - 2 * j)
    return (2 - swapped + RING) % RING


def loop(start, stop, body):
    def step(i, carry):
        body(i)
        return carry

    lax.fori_loop(start, stop, step, 0)


def down_kernel(
    hidden, w_hbm, o_ref, w, own, sib_out, sib_in, s1, r1, s2, r2, keep, fin,
    w_sem, sib_ss, sib_rs, ss1, rs1, ss2, rs2, fin_ss, fin_rs,
):
    y, z, core = place()
    half = hidden.shape[0] // 2
    quarter = half // 2
    columns = s2.shape[-1]
    w_copy = pltpu.make_async_copy(w_hbm, w, w_sem)
    w_copy.start()
    partners = [
        device((y + 1) % RING, z, core),
        device((y + 3) % RING, z, core),
        device(y, (z + 1) % RING, core),
        device(y, (z + 3) % RING, core),
        device(y, z, 1 - core),
    ]
    sibling = partners[-1]
    barrier = pltpu.get_barrier_semaphore()
    for partner in partners:
        pl.semaphore_signal(barrier, inc=1, device_id=partner, device_id_type=MESH)

    def product(role, first, second):
        py, pz = shifted(y, z, role, first, second)
        rows = pl.ds(pl.multiple_of(role * half, half), half)
        cols = pl.ds(pl.multiple_of((py * RING + pz) * columns, columns), columns)
        return jnp.dot(hidden[rows, :], w[:, cols], preferred_element_type=F32)

    def sib_copy(i):
        return pltpu.make_async_remote_copy(
            sib_out.at[i], sib_in.at[i], sib_ss.at[i], sib_rs.at[i],
            device_id=sibling, device_id_type=MESH,
        )

    def compute(slot, first, j):
        i = slot * RING + j
        sib_out[i] = product(1 - core, first, offset(j)).astype(BF16)
        sib_copy(i).start()
        own[i] = product(core, first, offset(j))

    def rows_of(s):
        return pl.ds(s * quarter, quarter)

    def total(slot, j, s):
        i = slot * RING + j
        return own[i, rows_of(s), :] + sib_in[i, rows_of(s), :].astype(F32)

    def copy1(kind, j):
        ty, tz = shifted(y, z, core, 1 if kind % 2 == 0 else 3, 0)
        return pltpu.make_async_remote_copy(
            s1.at[kind, j], r1.at[kind, j], ss1.at[kind, j], rs1.at[kind, j],
            device_id=device(ty, tz, core), device_id_type=MESH,
        )

    def copy2(kind):
        ty, tz = shifted(y, z, core, 0, 1 if kind % 2 == 0 else 3)
        return pltpu.make_async_remote_copy(
            s2.at[kind], r2.at[kind], ss2.at[kind], rs2.at[kind],
            device_id=device(ty, tz, core), device_id_type=MESH,
        )

    def finish_far(j):
        sib_copy(j).wait_recv()
        for d in range(2):
            s1[d, j] = total(0, j, d).astype(BF16)
            copy1(d, j).start()

    def finish_near(d, j):
        sib_copy((1 + d) * RING + j).wait_recv()
        s1[2 + d, j] = total(1 + d, j, 1 - d).astype(BF16)
        copy1(2 + d, j).start()

    def finish_relay(d, j):
        copy1(d, j).wait_recv()
        s1[4 + d, j] = (total(1 + d, j, d) + r1[d, j].astype(F32)).astype(BF16)
        copy1(4 + d, j).start()

    w_copy.wait()
    pl.semaphore_wait(barrier, len(partners))
    compute(0, 2, 0)

    def far(j):
        compute(0, 2, j)
        finish_far(j - 1)

    loop(1, RING, far)
    compute(1, 1, 0)
    finish_far(RING - 1)

    def near(j):
        compute(2, 3, j)
        finish_near(0, j)

        @pl.when(j < RING - 1)
        def _():
            compute(1, 1, j + 1)

        finish_near(1, j)

    loop(0, RING, near)

    def here(j):
        compute(3, 0, j)
        finish_relay(0, j)
        finish_relay(1, j)

    loop(0, RING, here)

    def summed(j):
        sib_copy(3 * RING + j).wait_recv()
        for kind in range(2, 6):
            copy1(kind, j).wait_recv()
        return (
            total(3, j, 0) + r1[4, j].astype(F32) + r1[3, j].astype(F32),
            total(3, j, 1) + r1[2, j].astype(F32) + r1[5, j].astype(F32),
        )

    parts = summed(0)
    for d in range(2):
        s2[d] = parts[d].astype(BF16)
        copy2(d).start()
    for d in range(2):
        parts = summed(1 + d)
        s2[2 + d] = parts[1 - d].astype(BF16)
        copy2(2 + d).start()
        keep[d] = parts[d]
    for d in range(2):
        copy2(d).wait_recv()
        s2[4 + d] = (keep[d] + r2[d].astype(F32)).astype(BF16)
        copy2(4 + d).start()
    parts = summed(3)
    for kind in range(2, 6):
        copy2(kind).wait_recv()
    final = jnp.concatenate(
        [
            parts[0] + r2[4].astype(F32) + r2[3].astype(F32),
            parts[1] + r2[2].astype(F32) + r2[5].astype(F32),
        ],
        axis=0,
    )
    left, right = final[:, : columns // 2], final[:, columns // 2 :]
    mine = pl.ds(pl.multiple_of(core * half, half), half)
    fin[...] = jnp.where(core == 0, right, left).astype(BF16)
    last = pltpu.make_async_remote_copy(
        fin, o_ref.at[mine], fin_ss, fin_rs, device_id=sibling, device_id_type=MESH
    )
    last.start()
    o_ref[mine, :] = jnp.where(core == 0, left, right).astype(BF16)

    def drain(j):
        for kind in range(6):
            copy1(kind, j).wait_send()
        for slot in range(4):
            sib_copy(slot * RING + j).wait_send()

    loop(0, RING, drain)
    for kind in range(6):
        copy2(kind).wait_send()
    last.wait()


def down(hidden, weights):
    tokens, units = hidden.shape
    width = weights.shape[1]
    columns = width // (RING * RING)
    half, quarter, blocks = tokens // 2, tokens // 4, RING * RING
    dma = pltpu.SemaphoreType.DMA
    return pl.pallas_call(
        down_kernel,
        out_shape=jax.ShapeDtypeStruct((tokens, columns // 2), BF16),
        in_specs=[pl.BlockSpec(memory_space=pltpu.VMEM), pl.BlockSpec(memory_space=pl.ANY)],
        out_specs=pl.BlockSpec(memory_space=pltpu.VMEM),
        scratch_shapes=[
            pltpu.VMEM((units, width), BF16),
            pltpu.VMEM((blocks, half, columns), F32),
            pltpu.VMEM((blocks, half, columns), BF16),
            pltpu.VMEM((blocks, half, columns), BF16),
            pltpu.VMEM((6, RING, quarter, columns), BF16),
            pltpu.VMEM((6, RING, quarter, columns), BF16),
            pltpu.VMEM((6, quarter, columns), BF16),
            pltpu.VMEM((6, quarter, columns), BF16),
            pltpu.VMEM((2, quarter, columns), F32),
            pltpu.VMEM((half, columns // 2), BF16),
            dma,
            dma((blocks,)),
            dma((blocks,)),
            dma((6, RING)),
            dma((6, RING)),
            dma((6,)),
            dma((6,)),
            dma,
            dma,
        ],
        name="down",
        compiler_params=pltpu.CompilerParams(
            collective_id=1, has_side_effects=True, vmem_limit_bytes=62 << 20
        ),
    )(hidden, weights)


def local(tokens, gain, up_weight, down_weight):
    gathered, gain_row = (
        lax.all_gather(tokens, "out", axis=1, tiled=True),
        lax.all_gather(gain, "out", axis=0, tiled=True),
    )
    values = gathered.astype(F32)
    totals = lax.psum((jnp.sum(values, axis=1), jnp.sum(values * values, axis=1)), "con")
    normed = normalize(values, totals, gain_row)
    partial_value = jnp.einsum("td,dgh->tgh", normed, up_weight, preferred_element_type=F32)
    summed = lax.psum_scatter(
        partial_value.astype(BF16), "con", scatter_dimension=1, tiled=True
    ).astype(F32)
    hidden = jax.nn.gelu(summed, approximate=False).astype(BF16)
    hidden = hidden.reshape(hidden.shape[0], hidden.shape[1] * hidden.shape[2])
    return down(hidden, down_weight)


def solution(mesh):
    in_specs = (
        P("tok", ("con", "out")),
        P(("con", "out")),
        P("con", None, "out"),
        P(("con", "out"), None),
    )
    out_specs = P("tok", ("con", "out"))
    return jax.shard_map(local, mesh=mesh, in_specs=in_specs, out_specs=out_specs, check_vma=False)
```

```python
import functools

import jax
import jax.numpy as jnp
from jax import lax
from jax.experimental import pallas as pl
from jax.experimental.pallas import tpu as pltpu
from jax.sharding import PartitionSpec as P

D = 10240
RING = 4
MESH = pl.DeviceIdType.MESH
F32, BF16 = jnp.float32, jnp.bfloat16


def place():
    con, out = lax.axis_index("con"), lax.axis_index("out")
    return con * 2 + out // 8, (out // 2) % RING, out % 2


def device(y, z, core):
    return (lax.axis_index("tok"), y // 2, (y % 2) * 8 + z * 2 + core)


def shifted(y, z, role, first, second):
    return (
        (y + first * role + second * (1 - role)) % RING,
        (z + first * (1 - role) + second * role) % RING,
    )


def offset(j):
    swapped = j + (j // 2) * (5 - 2 * j)
    return (2 - swapped + RING) % RING


def loop(start, stop, body):
    def step(i, carry):
        body(i)
        return carry

    lax.fori_loop(start, stop, step, 0)


def block_kernel(
    x_ref, xt_ref, gain_ref, u_hbm, w_hbm, o_ref,
    w, raw, sib_x, sib_xin, stat, stat_sib, stat_out, stat_in, blocks, normed, sib_normed, columns_of,
    acc, con_out, con_in, hidden, own, sib_out, sib_in, s1, r1, s2, r2, keep, fin,
    w_sem, raw_sem, sx_ss, sx_rs, sst_ss, sst_rs, st_ss, st_rs, bl_ss, bl_rs, nm_ss, nm_rs, con_ss, con_rs,
    sib_ss, sib_rs, ss1, rs1, ss2, rs2, fin_ss, fin_rs,
):
    y, z, core = place()
    con, low = y // 2, y % 2
    tokens, features = x_ref.shape
    half = tokens // 2
    quarter = half // 2
    columns = s2.shape[-1]
    chips = RING * RING
    sibling = device(y, z, 1 - core)
    mine = pl.ds(pl.multiple_of(core * half, half), half)
    theirs = pl.ds(pl.multiple_of((1 - core) * half, half), half)

    def remote(source, target, send, recv, where):
        return pltpu.make_async_remote_copy(
            source, target, send, recv, device_id=where, device_id_type=MESH
        )

    def raw_copy(b):
        rows = pl.ds(pl.multiple_of(b * columns, columns), columns)
        return pltpu.make_async_copy(u_hbm.at[rows], raw.at[b % 2], raw_sem.at[b % 2])

    raw_copy(0).start()
    barrier = pltpu.get_barrier_semaphore()
    pl.semaphore_signal(barrier, inc=1, device_id=sibling, device_id_type=MESH)

    def chip_at(q):
        return device((y + q // RING) % RING, (z + q) % RING, core)

    def greet(q):
        pl.semaphore_signal(barrier, inc=1, device_id=chip_at(q), device_id_type=MESH)

    loop(1, chips, greet)

    gain = jnp.broadcast_to(gain_ref[...], (16, features))
    sib_x[:half, :] = x_ref[theirs, :]
    sib_x[half:, :] = gain
    values = xt_ref[...].astype(F32)
    stat[0:1, :] = jnp.sum(values, axis=0, keepdims=True)
    stat[1:2, :] = jnp.sum(values * values, axis=0, keepdims=True)
    stat[2:8, :] = jnp.zeros((6, tokens), F32)
    pl.semaphore_wait(barrier, chips)
    stat_copy = remote(stat.at[:, theirs], stat_sib, sst_ss, sst_rs, sibling)
    stat_copy.start()
    x_copy = remote(sib_x, sib_xin, sx_ss, sx_rs, sibling)
    x_copy.start()
    stat_copy.wait_recv()
    stat_out[...] = stat[:, mine] + stat_sib[...]

    def stat_to(q):
        return remote(stat_out, stat_in.at[q], st_ss.at[q], st_rs.at[q], chip_at(q))

    loop(1, chips, lambda q: stat_to(q).start())
    x_copy.wait_recv()
    first = core == 0
    own_x, other_x = x_ref[mine, :], sib_xin[:half, :]
    other_gain = sib_xin[half:, :]
    blocks[0, :half, :] = jnp.concatenate(
        [jnp.where(first, own_x, other_x), jnp.where(first, other_x, own_x)], axis=1
    )
    blocks[0, half:, :] = jnp.concatenate(
        [jnp.where(first, gain, other_gain), jnp.where(first, other_gain, gain)], axis=1
    )

    routes = {1: (0, 1, 0), 2: (0, 0, 3), 4: (0, 0, 1), 3: (0, 0, 2), 5: (1, 0, 3), 7: (1, 0, 1), 6: (3, 1, 0)}

    def block_copy(n):
        source, dy, dz = routes[n]
        where = device(con * 2 + (low + dy) % 2, (z + dz) % RING, core)
        return remote(blocks.at[source], blocks.at[n], bl_ss.at[n], bl_rs.at[n], where)

    for n in (1, 2, 4, 3):
        block_copy(n).start()

    def unpack(b):
        @pl.when(b + 1 < 8)
        def _():
            raw_copy(b + 1).start()

        raw_copy(b).wait()

        def piece(r):
            rows = pl.ds(pl.multiple_of(r * 64, 64), 64)
            both = pltpu.einshape("khn->hkn", raw[b % 2, rows])
            w[2 * b, rows, :] = both[0]
            w[2 * b + 1, rows, :] = both[1]

        loop(0, columns // 64, piece)

    loop(0, 8, unpack)

    stat_in[0] = stat_out[...]
    loop(1, chips, lambda q: stat_to(q).wait_recv())
    sums = stat_in[0]
    for q in range(1, chips):
        sums = sums + stat_in[q]
    average = sums[0:1, :] / D
    scale = lax.rsqrt(sums[1:2, :] / D - average * average + 1e-05)
    columns_of[0] = jnp.broadcast_to(average, (128, half)).T
    columns_of[1] = jnp.broadcast_to(scale, (128, half)).T

    def normed_copy(n):
        return remote(normed.at[n], sib_normed.at[n], nm_ss.at[n], nm_rs.at[n], sibling)

    def normalize(n):
        gains = blocks[n, half : half + 1, :].astype(F32)

        def piece(r):
            rows = pl.ds(pl.multiple_of(r * 32, 32), 32)
            shape = (1, columns // 128)
            average = jnp.tile(columns_of[0, rows, :], shape)
            scale = jnp.tile(columns_of[1, rows, :], shape)
            values = blocks[n, rows, :].astype(F32)
            normed[n, rows, :] = ((values - average) * scale * gains).astype(BF16)

        loop(0, half // 32, piece)
        normed_copy(n).start()

    def weight_of(n):
        return (low + n // 5) % 2 * RING + (z + (n - 2) % 3 + 1) % RING

    def update(source, n, rows, block, part, start=False):
        term = jnp.dot(source[n], w[2 * block + part], preferred_element_type=F32)
        acc[part, rows, :] = term if start else acc[part, rows, :] + term

    here = low * RING + z
    beside = (1 - low) * RING + z
    normalize(0)
    for part in range(2):
        update(normed, 0, mine, here, part, True)
    block_copy(1).wait_recv()
    block_copy(5).start()
    block_copy(7).start()
    normalize(1)
    for part in range(2):
        update(normed, 1, mine, beside, part)
    normed_copy(0).wait_recv()
    for part in range(2):
        update(sib_normed, 0, theirs, here, part, True)
    normed_copy(1).wait_recv()
    for part in range(2):
        update(sib_normed, 1, theirs, beside, part)

    def arrived(n):
        remote(blocks.at[0], blocks.at[n], bl_ss.at[n], bl_rs.at[n], sibling).wait_recv()

    def take(n):
        arrived(n)

        @pl.when(n == 3)
        def _():
            block_copy(6).start()

        normalize(n)
        for part in range(2):
            update(normed, n, mine, weight_of(n), part)

        @pl.when(n > 2)
        def _():
            normed_copy(n - 1).wait_recv()
            for part in range(2):
                update(sib_normed, n - 1, theirs, weight_of(n - 1), part)

    loop(2, 7, take)

    partner = device((y + 2) % RING, z, core)
    last = 7

    def con_copy(k):
        return remote(con_out.at[k], con_in.at[k], con_ss.at[k], con_rs.at[k], partner)

    def give(k, source, rows):
        term = jnp.dot(source[last], w[2 * weight_of(last) + 1 - con], preferred_element_type=F32)
        con_out[k] = (acc[1 - con, rows, :] + term).astype(BF16)
        con_copy(k).start()

    arrived(last)
    normalize(last)
    give(0, normed, mine)
    normed_copy(last - 1).wait_recv()
    for part in range(2):
        update(sib_normed, last - 1, theirs, weight_of(last - 1), part)
    normed_copy(last).wait_recv()
    give(1, sib_normed, theirs)
    update(normed, last, mine, weight_of(last), con)
    update(sib_normed, last, theirs, weight_of(last), con)

    def w_copy(q):
        cols = pl.ds(pl.multiple_of(q * columns, columns), columns)
        return pltpu.make_async_copy(w_hbm.at[:, cols], w.at[q], w_sem.at[q])

    loop(0, chips, lambda q: w_copy(q).start())

    for k in range(2):
        con_copy(k).wait_recv()
        begin = (core + k) % 2 * half

        def activate(r, k=k, begin=begin):
            rows = pl.ds(pl.multiple_of(r * 32, 32), 32)
            whole = pl.ds(pl.multiple_of(begin + r * 32, 32), 32)
            v = acc[con, whole, :] + con_in[k, rows, :].astype(F32)
            hidden[whole, :] = (0.5 * v * (1.0 + lax.erf(v * (0.5**0.5)))).astype(BF16)

        loop(0, half // 32, activate)

    loop(0, chips, lambda q: w_copy(q).wait())

    def product(role, first, second):
        py, pz = shifted(y, z, role, first, second)
        rows = pl.ds(pl.multiple_of(role * half, half), half)
        return jnp.dot(hidden[rows, :], w[py * RING + pz], preferred_element_type=F32)

    def sib_copy(i):
        return pltpu.make_async_remote_copy(
            sib_out.at[i], sib_in.at[i], sib_ss.at[i], sib_rs.at[i],
            device_id=sibling, device_id_type=MESH,
        )

    def compute(slot, first, j):
        i = slot * RING + j
        sib_out[i] = product(1 - core, first, offset(j)).astype(BF16)
        sib_copy(i).start()
        own[slot % 3 * RING + j] = product(core, first, offset(j))

    def rows_of(s):
        return pl.ds(s * quarter, quarter)

    def total(slot, j, s):
        i = slot * RING + j
        return own[slot % 3 * RING + j, rows_of(s), :] + sib_in[i, rows_of(s), :].astype(F32)

    def copy1(kind, j):
        ty, tz = shifted(y, z, core, 1 if kind % 2 == 0 else 3, 0)
        return pltpu.make_async_remote_copy(
            s1.at[kind, j], r1.at[kind, j], ss1.at[kind, j], rs1.at[kind, j],
            device_id=device(ty, tz, core), device_id_type=MESH,
        )

    def copy2(kind):
        ty, tz = shifted(y, z, core, 0, 1 if kind % 2 == 0 else 3)
        return pltpu.make_async_remote_copy(
            s2.at[kind], r2.at[kind], ss2.at[kind], rs2.at[kind],
            device_id=device(ty, tz, core), device_id_type=MESH,
        )

    def finish_far(j):
        sib_copy(j).wait_recv()
        for d in range(2):
            s1[d, j] = total(0, j, d).astype(BF16)
            copy1(d, j).start()

    def finish_near(d, j):
        sib_copy((1 + d) * RING + j).wait_recv()
        s1[2 + d, j] = total(1 + d, j, 1 - d).astype(BF16)
        copy1(2 + d, j).start()

    def finish_relay(d, j):
        copy1(d, j).wait_recv()
        s1[4 + d, j] = (total(1 + d, j, d) + r1[d, j].astype(F32)).astype(BF16)
        copy1(4 + d, j).start()

    compute(0, 2, 0)

    def far(j):
        compute(0, 2, j)
        finish_far(j - 1)

    loop(1, RING, far)
    compute(1, 1, 0)
    finish_far(RING - 1)

    def near(j):
        compute(2, 3, j)
        finish_near(0, j)

        @pl.when(j < RING - 1)
        def _():
            compute(1, 1, j + 1)

        finish_near(1, j)

    loop(0, RING, near)

    def at_home(j):
        compute(3, 0, j)
        finish_relay(0, j)
        finish_relay(1, j)

    loop(0, RING, at_home)

    def summed(j):
        sib_copy(3 * RING + j).wait_recv()
        for kind in range(2, 6):
            copy1(kind, j).wait_recv()
        return (
            total(3, j, 0) + r1[4, j].astype(F32) + r1[3, j].astype(F32),
            total(3, j, 1) + r1[2, j].astype(F32) + r1[5, j].astype(F32),
        )

    parts = summed(0)
    for d in range(2):
        s2[d] = parts[d].astype(BF16)
        copy2(d).start()
    for d in range(2):
        parts = summed(1 + d)
        s2[2 + d] = parts[1 - d].astype(BF16)
        copy2(2 + d).start()
        keep[d] = parts[d]
    for d in range(2):
        copy2(d).wait_recv()
        s2[4 + d] = (keep[d] + r2[d].astype(F32)).astype(BF16)
        copy2(4 + d).start()
    parts = summed(3)
    for kind in range(2, 6):
        copy2(kind).wait_recv()
    final = jnp.concatenate(
        [
            parts[0] + r2[4].astype(F32) + r2[3].astype(F32),
            parts[1] + r2[2].astype(F32) + r2[5].astype(F32),
        ],
        axis=0,
    )
    left, right = final[:, : columns // 2], final[:, columns // 2 :]
    fin[...] = jnp.where(core == 0, right, left).astype(BF16)
    final_copy = pltpu.make_async_remote_copy(
        fin, o_ref.at[mine], fin_ss, fin_rs, device_id=sibling, device_id_type=MESH
    )
    final_copy.start()
    o_ref[mine, :] = jnp.where(core == 0, left, right).astype(BF16)

    def drain(j):
        for kind in range(6):
            copy1(kind, j).wait_send()
        for slot in range(4):
            sib_copy(slot * RING + j).wait_send()

    loop(0, RING, drain)
    for kind in range(6):
        copy2(kind).wait_send()
    final_copy.wait()
    stat_copy.wait_send()
    x_copy.wait_send()
    loop(1, chips, lambda q: stat_to(q).wait_send())
    for n in range(1, 8):
        block_copy(n).wait_send()
    loop(0, 8, lambda n: normed_copy(n).wait_send())
    for k in range(2):
        con_copy(k).wait_send()


def local(tokens, gain, up_weight, down_weight):
    count, features = tokens.shape
    depth = up_weight.shape[0]
    units, width = down_weight.shape
    chips = RING * RING
    columns = width // chips
    half, quarter = count // 2, count // 4
    dma = pltpu.SemaphoreType.DMA
    vmem = pl.BlockSpec(memory_space=pltpu.VMEM)
    hbm = pl.BlockSpec(memory_space=pl.ANY)
    return pl.pallas_call(
        block_kernel,
        out_shape=jax.ShapeDtypeStruct((count, width // chips // 2), BF16),
        in_specs=[vmem, vmem, vmem, hbm, hbm],
        out_specs=vmem,
        scratch_shapes=[
            pltpu.VMEM((chips, columns, columns), BF16),
            pltpu.VMEM((2, columns, 2, units), BF16),
            pltpu.VMEM((half + 16, features), BF16),
            pltpu.VMEM((half + 16, features), BF16),
            pltpu.VMEM((8, count), F32),
            pltpu.VMEM((8, half), F32),
            pltpu.VMEM((8, half), F32),
            pltpu.VMEM((chips, 8, half), F32),
            pltpu.VMEM((8, half + 16, columns), BF16),
            pltpu.VMEM((8, half, columns), BF16),
            pltpu.VMEM((8, half, columns), BF16),
            pltpu.VMEM((2, half, 128), F32),
            pltpu.VMEM((2, count, units), F32),
            pltpu.VMEM((2, half, units), BF16),
            pltpu.VMEM((2, half, units), BF16),
            pltpu.VMEM((count, units), BF16),
            pltpu.VMEM((3 * RING, half, columns), F32),
            pltpu.VMEM((chips, half, columns), BF16),
            pltpu.VMEM((chips, half, columns), BF16),
            pltpu.VMEM((6, RING, quarter, columns), BF16),
            pltpu.VMEM((6, RING, quarter, columns), BF16),
            pltpu.VMEM((6, quarter, columns), BF16),
            pltpu.VMEM((6, quarter, columns), BF16),
            pltpu.VMEM((2, quarter, columns), F32),
            pltpu.VMEM((half, columns // 2), BF16),
            dma((chips,)), dma((2,)), dma, dma, dma, dma, dma((chips,)), dma((chips,)),
            dma((8,)), dma((8,)), dma((8,)), dma((8,)), dma((2,)), dma((2,)),
            dma((chips,)), dma((chips,)), dma((6, RING)), dma((6, RING)), dma((6,)), dma((6,)), dma, dma,
        ],
        name="block",
        compiler_params=pltpu.CompilerParams(
            collective_id=1, has_side_effects=True, vmem_limit_bytes=62 << 20
        ),
    )(tokens, tokens.T, gain.reshape(1, features), up_weight, down_weight)


def solution(mesh):
    in_specs = (
        P("tok", ("con", "out")),
        P(("con", "out")),
        P("con", None, "out"),
        P(("con", "out"), None),
    )
    out_specs = P("tok", ("con", "out"))
    return jax.shard_map(local, mesh=mesh, in_specs=in_specs, out_specs=out_specs, check_vma=False)
```

```python
import functools

import jax
import jax.numpy as jnp
from jax import lax
from jax.experimental import pallas as pl
from jax.experimental.pallas import tpu as pltpu
from jax.sharding import PartitionSpec as P

D = 10240
RING = 4
MESH = pl.DeviceIdType.MESH
F32, BF16 = jnp.float32, jnp.bfloat16


def place():
    con, out = lax.axis_index("con"), lax.axis_index("out")
    return con * 2 + out // 8, (out // 2) % RING, out % 2


def device(y, z, core):
    return (lax.axis_index("tok"), y // 2, (y % 2) * 8 + z * 2 + core)


def shifted(y, z, role, first, second):
    return (
        (y + first * role + second * (1 - role)) % RING,
        (z + first * (1 - role) + second * role) % RING,
    )


def offset(j):
    swapped = j + (j // 2) * (5 - 2 * j)
    return (2 - swapped + RING) % RING


def loop(start, stop, body):
    def step(i, carry):
        body(i)
        return carry

    lax.fori_loop(start, stop, step, 0)


def block_kernel(
    xt_hbm, gain_ref, u_hbm, w_hbm, o_ref,
    xt_ref, w, raw, sib_xt, tall, own_gain, sib_gain, stat_out, stat_in, blocks, normed, columns_of,
    acc, con_out, con_in, hidden, own, sib_out, sib_in, s1, r1, s2, r2, fin,
    xt_sem, w_sem, raw_sem, sx_ss, sx_rs, sg_ss, sg_rs, st_ss, st_rs, bl_ss, bl_rs, nm_ss, nm_rs, con_ss, con_rs,
    sib_ss, sib_rs, ss1, rs1, ss2, rs2, fin_ss, fin_rs,
):
    y, z, core = place()
    con, low = y // 2, y % 2
    features, tokens = xt_ref.shape
    half = tokens // 2
    quarter = half // 2
    columns = s2.shape[-1]
    chips = RING * RING
    sibling = device(y, z, 1 - core)
    mine = pl.ds(pl.multiple_of(core * half, half), half)
    theirs = pl.ds(pl.multiple_of((1 - core) * half, half), half)
    my_quarter = pl.ds(pl.multiple_of(core * quarter, quarter), quarter)

    def remote(source, target, send, recv, where):
        return pltpu.make_async_remote_copy(
            source, target, send, recv, device_id=where, device_id_type=MESH
        )

    def raw_copy(b):
        rows = pl.ds(pl.multiple_of(b * columns, columns), columns)
        return pltpu.make_async_copy(u_hbm.at[rows], raw.at[b % 2], raw_sem.at[b % 2])

    xt_copy = pltpu.make_async_copy(xt_hbm, xt_ref, xt_sem)
    xt_copy.start()
    raw_copy(0).start()
    barrier = pltpu.get_barrier_semaphore()
    pl.semaphore_signal(barrier, inc=1, device_id=sibling, device_id_type=MESH)

    def chip_at(q):
        return device((y + q // RING) % RING, (z + q) % RING, core)

    def greet(q):
        pl.semaphore_signal(barrier, inc=1, device_id=chip_at(q), device_id_type=MESH)

    loop(1, chips, greet)

    gain = gain_ref[...].astype(F32).reshape(1, features)
    own_gain[...] = jnp.broadcast_to(gain, (8, features))
    xt_copy.wait()
    tall[pl.ds(pl.multiple_of(core * features, features), features), :] = xt_ref[:, mine]
    stat_out[...] = jnp.zeros(stat_out.shape, F32)
    pl.semaphore_wait(barrier, chips)
    x_copy = remote(xt_ref.at[:, theirs], sib_xt, sx_ss, sx_rs, sibling)
    x_copy.start()
    gain_copy = remote(own_gain, sib_gain, sg_ss, sg_rs, sibling)
    gain_copy.start()
    x_copy.wait_recv()
    tall[pl.ds(pl.multiple_of((1 - core) * features, features), features), :] = sib_xt[...]
    for c in range(columns // 128):
        lanes = slice(c * 128, (c + 1) * 128)
        blocks[0, :, lanes] = tall[lanes, :].T

    routes = {4: (0, 1, 0), 1: (0, 0, 3), 3: (0, 0, 1), 2: (0, 0, 2), 5: (4, 0, 3), 7: (4, 0, 1)}

    def block_copy(n, s):
        source, dy, dz = routes[n] if n != 6 else ((2, 1, 0), (4, 0, 2))[s]
        rows = pl.ds(s * quarter, quarter)
        where = device(con * 2 + (low + dy) % 2, (z + dz) % RING, core)
        return remote(
            blocks.at[source, rows], blocks.at[n, rows], bl_ss.at[n, s], bl_rs.at[n, s], where
        )

    def arrived(n, s):
        rows = pl.ds(s * quarter, quarter)
        remote(
            blocks.at[0, rows], blocks.at[n, rows], bl_ss.at[n, s], bl_rs.at[n, s], sibling
        ).wait_recv()

    for n in (4, 1, 3, 2):
        block_copy(n, 0).start()

    values = tall[...].astype(F32)
    sums = jnp.sum(values, axis=0, keepdims=True)
    squares = jnp.sum(values * values, axis=0, keepdims=True)
    gain_copy.wait_recv()
    first = core == 0
    other_gain = sib_gain[0:1, :]
    chip_gain = jnp.concatenate(
        [jnp.where(first, gain, other_gain), jnp.where(first, other_gain, gain)], axis=1
    )
    for k in range(half // 128):
        lanes = slice(k * 128, (k + 1) * 128)
        stat_out[k : k + 1, :] = sums[:, lanes]
        stat_out[2 + k : 3 + k, :] = squares[:, lanes]
    for k in range(columns // 128):
        stat_out[8 + k : 9 + k, :] = chip_gain[:, k * 128 : (k + 1) * 128]

    def stat_to(q):
        where = device((y + RING - q // RING) % RING, (z + chips - q) % RING, core)
        return remote(stat_out, stat_in.at[q], st_ss.at[q], st_rs.at[q], where)

    loop(1, chips, lambda q: stat_to(q).start())

    def unpack(b):
        @pl.when(b + 1 < 8)
        def _():
            raw_copy(b + 1).start()

        raw_copy(b).wait()

        def piece(r):
            rows = pl.ds(pl.multiple_of(r * 64, 64), 64)
            both = pltpu.einshape("khn->hkn", raw[b % 2, rows])
            w[2 * b, rows, :] = both[0]
            w[2 * b + 1, rows, :] = both[1]

        loop(0, columns // 64, piece)

    loop(0, 2, unpack)
    arrived(4, 0)
    block_copy(5, 0).start()
    block_copy(7, 0).start()
    block_copy(4, 1).start()
    loop(2, 5, unpack)
    arrived(2, 0)
    block_copy(6, 0).start()
    for n in (1, 3, 2):
        block_copy(n, 1).start()
    loop(5, 8, unpack)

    stat_in[0] = stat_out[...]
    loop(1, chips, lambda q: stat_to(q).wait_recv())
    whole = stat_in[0]
    for q in range(1, chips):
        whole = whole + stat_in[q]
    average = whole[0:2, :] / D
    scale = lax.rsqrt(whole[2:4, :] / D - average * average + 1e-05)
    for k in range(2):
        rows = slice(k * 128, (k + 1) * 128)
        columns_of[0, rows, :] = jnp.broadcast_to(average[k : k + 1, :], (128, 128)).T
        columns_of[1, rows, :] = jnp.broadcast_to(scale[k : k + 1, :], (128, 128)).T

    def weight_of(n):
        return (low + n // RING) % 2 * RING + (z + n) % RING

    def normed_copy(n, s):
        return remote(
            normed.at[n, s, my_quarter], normed.at[n, s, my_quarter], nm_ss.at[n, s], nm_rs.at[n, s], sibling
        )

    def normed_arrived(n, s):
        rows = pl.ds(pl.multiple_of((1 - core) * quarter, quarter), quarter)
        remote(
            normed.at[n, s, rows], normed.at[n, s, rows], nm_ss.at[n, s], nm_rs.at[n, s], sibling
        ).wait_recv()

    def normalize(n, s):
        seen = (n // RING * (1 - 2 * low) + RING) % RING * RING + n % RING
        gains = jnp.concatenate(
            [stat_in[seen, 8 + k : 9 + k, :] for k in range(columns // 128)], axis=1
        )

        def piece(r):
            rows = pl.ds(pl.multiple_of(s * quarter + r * 32, 32), 32)
            shape = (1, columns // 128)
            average = jnp.tile(columns_of[0, rows, :], shape)
            scale = jnp.tile(columns_of[1, rows, :], shape)
            values = blocks[n, rows, :].astype(F32)
            place_to = pl.ds(pl.multiple_of(core * quarter + r * 32, 32), 32)
            normed[n, s, place_to, :] = ((values - average) * scale * gains).astype(BF16)

        loop(0, quarter // 32, piece)
        normed_copy(n, s).start()

    def w_copy(q):
        cols = pl.ds(pl.multiple_of(q * columns, columns), columns)
        return pltpu.make_async_copy(w_hbm.at[:, cols], w.at[q], w_sem.at[q])

    def release(n):
        for part in range(2):
            w_copy(2 * weight_of(n) + part).start()

    def update(n, s, part, start=False):
        term = jnp.dot(normed[n, s], w[2 * weight_of(n) + part], preferred_element_type=F32)
        acc[part, s] = term if start else acc[part, s] + term

    partner = device((y + 2) % RING, z, core)

    def con_copy(s):
        return remote(con_out.at[s], con_in.at[s], con_ss.at[s], con_rs.at[s], partner)

    def up(s):
        normalize(0, s)
        arrived(1, s)
        if s == 0:
            arrived(4, 1)
            for n in (5, 7, 6):
                block_copy(n, 1).start()
        normalize(1, s)
        normed_arrived(0, s)
        for part in range(2):
            update(0, s, part, True)
        if s == 1:
            release(0)

        def take(n):
            @pl.when((n != 4) & ((n != 2) | (s == 1)))
            def _():
                arrived(n, s)

            normalize(n, s)
            normed_arrived(n - 1, s)
            for part in range(2):
                update(n - 1, s, part)
            if s == 1:
                release(n - 1)

        loop(2, 8, take)
        normed_arrived(7, s)
        term = jnp.dot(normed[7, s], w[2 * weight_of(7) + 1 - con], preferred_element_type=F32)
        con_out[s] = (acc[1 - con, s] + term).astype(BF16)
        con_copy(s).start()
        update(7, s, con)
        if s == 1:
            release(7)

    def activate(s):
        con_copy(s).wait_recv()

        def piece(r):
            rows = pl.ds(pl.multiple_of(r * 32, 32), 32)
            v = acc[con, s, rows, :] + con_in[s, rows, :].astype(F32)
            hidden[s, rows, :] = (0.5 * v * (1.0 + lax.erf(v * (0.5**0.5)))).astype(BF16)

        loop(0, half // 32, piece)

    def product(role, first, second, s):
        py, pz = shifted(y, z, role, first, second)
        rows = pl.ds(pl.multiple_of(role * quarter, quarter), quarter)
        return jnp.dot(hidden[s, rows, :], w[py * RING + pz], preferred_element_type=F32)

    def sib_copy(t, s):
        return remote(sib_out.at[t, s], sib_in.at[t, s], sib_ss.at[t, s], sib_rs.at[t, s], sibling)

    def slot(t, s):
        return t + t // (2 * RING) * 2 * RING * s

    def total(t, s):
        return own[slot(t, s)] + sib_in[t, s].astype(F32)

    def copy1(kind, j):
        ty, tz = shifted(y, z, core, 1 if kind % 2 == 0 else 3, 0)
        return remote(s1.at[kind, j], r1.at[kind, j], ss1.at[kind, j], rs1.at[kind, j], device(ty, tz, core))

    def copy2(s, j):
        ty, tz = shifted(y, z, core, 0, offset(j))
        return remote(s2.at[s, j], r2.at[s, j], ss2.at[s, j], rs2.at[s, j], device(ty, tz, core))

    def compute(t, s):
        group, second = t // RING, offset(t % RING)
        first = offset(group) if s == 1 else (RING - offset(group)) % RING
        sib_out[t, s] = product(1 - core, first, second, s).astype(BF16)
        sib_copy(t, s).start()
        own[slot(t, s)] = product(core, first, second, s)

    def send_direct(t, s):
        sib_copy(t, s).wait_recv()

        @pl.when(t < RING)
        def _():
            s1[s, t] = total(t, s).astype(BF16)
            copy1(s, t).start()

        @pl.when(t >= RING)
        def _():
            s1[3 - s, t - RING] = total(t, s).astype(BF16)
            copy1(3 - s, t - RING).start()

    def direct(s):
        compute(0, s)

        def step(t):
            compute(t, s)
            send_direct(t - 1, s)

        loop(1, 2 * RING, step)
        compute(2 * RING, s)
        send_direct(2 * RING - 1, s)

    def relay(s):
        def step(j):
            t = 2 * RING + j
            sib_copy(t, s).wait_recv()
            copy1(s, j).wait_recv()
            s1[4 + s, j] = (total(t, s) + r1[s, j].astype(F32)).astype(BF16)
            copy1(4 + s, j).start()

        loop(0, RING, step)

    up(0)
    up(1)
    activate(0)
    loop(0, chips, lambda q: w_copy(q).wait())
    direct(0)
    loop(2 * RING + 1, 3 * RING, lambda t: compute(t, 0))
    activate(1)
    direct(1)
    relay(0)
    loop(2 * RING + 1, 3 * RING, lambda t: compute(t, 1))
    loop(3 * RING, chips, lambda t: compute(t, 0))
    loop(3 * RING, chips, lambda t: compute(t, 1))
    relay(1)

    def summed(j, s):
        sib_copy(3 * RING + j, s).wait_recv()
        copy1(3 - s, j).wait_recv()
        copy1(4 + s, j).wait_recv()
        return total(3 * RING + j, s) + r1[4 + s, j].astype(F32) + r1[3 - s, j].astype(F32)

    for s in range(2):
        for j in range(3):
            s2[s, j] = summed(j, s).astype(BF16)
            copy2(s, j).start()
    final_copies = []
    for s in range(2):
        final = summed(3, s)
        for j in range(3):
            copy2(s, j).wait_recv()
            final = final + r2[s, j].astype(F32)
        left, right = final[:, : columns // 2], final[:, columns // 2 :]
        fin[s] = jnp.where(core == 0, right, left).astype(BF16)
        rows = pl.ds(pl.multiple_of(core * half + s * quarter, quarter), quarter)
        final_copy = remote(fin.at[s], o_ref.at[rows], fin_ss.at[s], fin_rs.at[s], sibling)
        final_copy.start()
        final_copies.append(final_copy)
        o_ref[rows, :] = jnp.where(core == 0, left, right).astype(BF16)

    def drain(j):
        for kind in range(6):
            copy1(kind, j).wait_send()
        for group in range(4):
            for s in range(2):
                sib_copy(group * RING + j, s).wait_send()

    loop(0, RING, drain)
    for s in range(2):
        for j in range(3):
            copy2(s, j).wait_send()
        final_copies[s].wait()
    x_copy.wait_send()
    gain_copy.wait_send()
    loop(1, chips, lambda q: stat_to(q).wait_send())
    for s in range(2):
        for n in range(1, 8):
            block_copy(n, s).wait_send()
        for n in range(8):
            normed_copy(n, s).wait_send()
        con_copy(s).wait_send()


def local(tokens, gain, up_weight, down_weight):
    count, features = tokens.shape
    units, width = down_weight.shape
    chips = RING * RING
    columns = width // chips
    half, quarter = count // 2, count // 4
    dma = pltpu.SemaphoreType.DMA
    vmem = pl.BlockSpec(memory_space=pltpu.VMEM)
    hbm = pl.BlockSpec(memory_space=pl.ANY)
    return pl.pallas_call(
        block_kernel,
        out_shape=jax.ShapeDtypeStruct((count, columns // 2), BF16),
        in_specs=[hbm, vmem, hbm, hbm],
        out_specs=vmem,
        scratch_shapes=[
            pltpu.VMEM((features, count), BF16),
            pltpu.VMEM((chips, columns, columns), BF16),
            pltpu.VMEM((2, columns, 2, units), BF16),
            pltpu.VMEM((features, half), BF16),
            pltpu.VMEM((columns, half), BF16),
            pltpu.VMEM((8, features), F32),
            pltpu.VMEM((8, features), F32),
            pltpu.VMEM((16, 128), F32),
            pltpu.VMEM((chips, 16, 128), F32),
            pltpu.VMEM((8, half, columns), BF16),
            pltpu.VMEM((8, 2, half, columns), BF16),
            pltpu.VMEM((2, half, 128), F32),
            pltpu.VMEM((2, 2, half, units), F32),
            pltpu.VMEM((2, half, units), BF16),
            pltpu.VMEM((2, half, units), BF16),
            pltpu.VMEM((2, half, units), BF16),
            pltpu.VMEM((6 * RING, quarter, columns), F32),
            pltpu.VMEM((chips, 2, quarter, columns), BF16),
            pltpu.VMEM((chips, 2, quarter, columns), BF16),
            pltpu.VMEM((6, RING, quarter, columns), BF16),
            pltpu.VMEM((6, RING, quarter, columns), BF16),
            pltpu.VMEM((2, 3, quarter, columns), BF16),
            pltpu.VMEM((2, 3, quarter, columns), BF16),
            pltpu.VMEM((2, quarter, columns // 2), BF16),
            dma, dma((chips,)), dma((2,)), dma, dma, dma, dma, dma((chips,)), dma((chips,)),
            dma((8, 2)), dma((8, 2)), dma((8, 2)), dma((8, 2)), dma((2,)), dma((2,)),
            dma((chips, 2)), dma((chips, 2)), dma((6, RING)), dma((6, RING)), dma((2, 3)), dma((2, 3)), dma((2,)), dma((2,)),
        ],
        name="block",
        compiler_params=pltpu.CompilerParams(
            collective_id=1, has_side_effects=True, vmem_limit_bytes=62 << 20
        ),
    )(tokens.T, gain, up_weight, down_weight)


def solution(mesh):
    in_specs = (
        P("tok", ("con", "out")),
        P(("con", "out")),
        P("con", None, "out"),
        P(("con", "out"), None),
    )
    out_specs = P("tok", ("con", "out"))
    return jax.shard_map(local, mesh=mesh, in_specs=in_specs, out_specs=out_specs, check_vma=False)
```

```python
import functools

import jax
import jax.numpy as jnp
from jax import lax
from jax.experimental import pallas as pl
from jax.experimental.pallas import tpu as pltpu
from jax.sharding import PartitionSpec as P

D = 10240
RING = 4
FIRST = 160
MESH = pl.DeviceIdType.MESH
F32, BF16 = jnp.float32, jnp.bfloat16


def place():
    con, out = lax.axis_index("con"), lax.axis_index("out")
    return con * 2 + out // 8, (out // 2) % RING, out % 2


def device(y, z, core):
    return (lax.axis_index("tok"), y // 2, (y % 2) * 8 + z * 2 + core)


def shifted(y, z, role, first, second):
    return (
        (y + first * role + second * (1 - role)) % RING,
        (z + first * (1 - role) + second * role) % RING,
    )


def offset(j):
    swapped = j + (j // 2) * (5 - 2 * j)
    return (2 - swapped + RING) % RING


def loop(start, stop, body):
    def step(i, carry):
        body(i)
        return carry

    lax.fori_loop(start, stop, step, 0)


def block_kernel(
    xt_hbm, gain_ref, u_hbm, w_hbm, o_ref,
    xt_ref, w, raw, sib_xt, tall, own_gain, sib_gain, stat_out, stat_in, blocks, normed, columns_of,
    acc, con_out, con_in, hidden, own, sib_out, sib_in, s1, r1, s2, r2, fin,
    xt_sem, w_sem, raw_sem, sx_ss, sx_rs, sg_ss, sg_rs, st_ss, st_rs, bl_ss, bl_rs, nm_ss, nm_rs, con_ss, con_rs,
    sib_ss, sib_rs, ss1, rs1, ss2, rs2, fin_ss, fin_rs,
):
    y, z, core = place()
    con, low = y // 2, y % 2
    features, tokens = xt_ref.shape
    half = tokens // 2
    quarter = half // 2
    columns = tall.shape[0]
    chips = RING * RING
    sibling = device(y, z, 1 - core)
    mine = pl.ds(pl.multiple_of(core * half, half), half)
    theirs = pl.ds(pl.multiple_of((1 - core) * half, half), half)
    my_quarter = pl.ds(pl.multiple_of(core * quarter, quarter), quarter)

    def remote(source, target, send, recv, where):
        return pltpu.make_async_remote_copy(
            source, target, send, recv, device_id=where, device_id_type=MESH
        )

    def raw_copy(b):
        rows = pl.ds(pl.multiple_of(b * columns, columns), columns)
        return pltpu.make_async_copy(u_hbm.at[rows], raw.at[b % 2], raw_sem.at[b % 2])

    xt_copy = pltpu.make_async_copy(xt_hbm, xt_ref, xt_sem)
    xt_copy.start()
    for b in range(2):
        raw_copy(b).start()
    barrier = pltpu.get_barrier_semaphore()
    pl.semaphore_signal(barrier, inc=1, device_id=sibling, device_id_type=MESH)

    def chip_at(q):
        return device((y + q // RING) % RING, (z + q) % RING, core)

    def greet(q):
        pl.semaphore_signal(barrier, inc=1, device_id=chip_at(q), device_id_type=MESH)

    loop(1, chips, greet)

    gain = gain_ref[...].astype(F32).reshape(1, features)
    own_gain[...] = jnp.broadcast_to(gain, (8, features))
    xt_copy.wait()
    tall[pl.ds(pl.multiple_of(core * features, features), features), :] = xt_ref[:, mine]
    stat_out[...] = jnp.zeros(stat_out.shape, F32)
    pl.semaphore_wait(barrier, chips)
    x_copy = remote(xt_ref.at[:, theirs], sib_xt, sx_ss, sx_rs, sibling)
    x_copy.start()
    gain_copy = remote(own_gain, sib_gain, sg_ss, sg_rs, sibling)
    gain_copy.start()
    def unpack(b):
        n = (b // RING + low) % 2 * RING + (b - z + RING) % RING
        raw_copy(b).wait()

        def piece(r):
            rows = pl.ds(pl.multiple_of(r * 64, 64), 64)
            both = pltpu.einshape("khn->hkn", raw[b % 2, rows])
            rows = pl.ds(pl.multiple_of(n % 2 * columns + r * 64, 64), 64)
            w[n // 2, rows, :columns] = both[0]
            w[n // 2, rows, columns:] = both[1]

        loop(0, columns // 64, piece)

        @pl.when(b + 2 < 8)
        def _():
            raw_copy(b + 2).start()

    loop(0, 2, unpack)
    x_copy.wait_recv()
    tall[pl.ds(pl.multiple_of((1 - core) * features, features), features), :] = sib_xt[...]
    for c in range(columns // 128):
        lanes = slice(c * 128, (c + 1) * 128)
        blocks[0, :, lanes] = tall[lanes, :].T

    routes = {4: (0, 1, 0), 1: (0, 0, 3), 3: (0, 0, 1), 2: (0, 0, 2), 5: (4, 0, 3), 7: (4, 0, 1)}

    def block_copy(n, s):
        source, dy, dz = routes[n] if n != 6 else ((2, 1, 0), (4, 0, 2))[s]
        rows = pl.ds(s * quarter, quarter)
        where = device(con * 2 + (low + dy) % 2, (z + dz) % RING, core)
        return remote(
            blocks.at[source, rows], blocks.at[n, rows], bl_ss.at[n, s], bl_rs.at[n, s], where
        )

    def arrived(n, s):
        rows = pl.ds(s * quarter, quarter)
        remote(
            blocks.at[0, rows], blocks.at[n, rows], bl_ss.at[n, s], bl_rs.at[n, s], sibling
        ).wait_recv()

    for n in (4, 1, 3, 2):
        block_copy(n, 0).start()

    values = tall[...].astype(F32)
    sums = jnp.sum(values, axis=0, keepdims=True)
    squares = jnp.sum(values * values, axis=0, keepdims=True)
    gain_copy.wait_recv()
    first = core == 0
    other_gain = sib_gain[0:1, :]
    chip_gain = jnp.concatenate(
        [jnp.where(first, gain, other_gain), jnp.where(first, other_gain, gain)], axis=1
    )
    for k in range(half // 128):
        lanes = slice(k * 128, (k + 1) * 128)
        stat_out[k : k + 1, :] = sums[:, lanes]
        stat_out[2 + k : 3 + k, :] = squares[:, lanes]
    for k in range(columns // 128):
        stat_out[8 + k : 9 + k, :] = chip_gain[:, k * 128 : (k + 1) * 128]

    def stat_to(q):
        where = device((y + RING - q // RING) % RING, (z + chips - q) % RING, core)
        return remote(stat_out, stat_in.at[q], st_ss.at[q], st_rs.at[q], where)

    loop(1, chips, lambda q: stat_to(q).start())

    loop(2, 4, unpack)
    arrived(4, 0)
    block_copy(5, 0).start()
    block_copy(7, 0).start()
    block_copy(4, 1).start()
    loop(4, 8, unpack)

    stat_in[0] = stat_out[...]
    loop(1, chips, lambda q: stat_to(q).wait_recv())
    whole = stat_in[0]
    for q in range(1, chips):
        whole = whole + stat_in[q]
    average = whole[0:2, :] / D
    scale = lax.rsqrt(whole[2:4, :] / D - average * average + 1e-05)
    for k in range(2):
        rows = slice(k * 128, (k + 1) * 128)
        columns_of[0, rows, :] = jnp.broadcast_to(average[k : k + 1, :], (128, 128)).T
        columns_of[1, rows, :] = jnp.broadcast_to(scale[k : k + 1, :], (128, 128)).T

    arrived(2, 0)
    block_copy(6, 0).start()
    for n in (1, 3, 2):
        block_copy(n, 1).start()

    def pair_rows(n, s, c):
        rows = pl.ds(pl.multiple_of(c * quarter, quarter), quarter)
        return normed.at[n // 2, s, rows, pl.ds(pl.multiple_of(n % 2 * columns, columns), columns)]

    def normed_copy(n, s):
        part = pair_rows(n, s, core)
        return remote(part, part, nm_ss.at[n, s], nm_rs.at[n, s], sibling)

    def normed_arrived(n, s):
        part = pair_rows(n, s, 1 - core)
        remote(part, part, nm_ss.at[n, s], nm_rs.at[n, s], sibling).wait_recv()

    def normalize(n, s):
        seen = (n // RING * (1 - 2 * low) + RING) % RING * RING + n % RING
        gains = jnp.concatenate(
            [stat_in[seen, 8 + k : 9 + k, :] for k in range(columns // 128)], axis=1
        )

        def piece(r):
            rows = pl.ds(pl.multiple_of(s * quarter + r * 32, 32), 32)
            shape = (1, columns // 128)
            average = jnp.tile(columns_of[0, rows, :], shape)
            scale = jnp.tile(columns_of[1, rows, :], shape)
            values = blocks[n, rows, :].astype(F32)
            place_to = pl.ds(pl.multiple_of(core * quarter + r * 32, 32), 32)
            part = pl.ds(pl.multiple_of(n % 2 * columns, columns), columns)
            normed[n // 2, s, place_to, part] = ((values - average) * scale * gains).astype(BF16)

        loop(0, quarter // 32, piece)
        normed_copy(n, s).start()

    def down_block(q):
        rows = pl.ds(pl.multiple_of(q // 2 % 2 * columns, columns), columns)
        return w.at[q // RING, rows, pl.ds(pl.multiple_of(q % 2 * columns, columns), columns)]

    def w_copy(q):
        cols = pl.ds(pl.multiple_of(q * columns, columns), columns)
        return pltpu.make_async_copy(w_hbm.at[:, cols], down_block(q), w_sem.at[q])

    def release(pair):
        for k in range(RING):
            w_copy(pair * RING + k).start()

    partner = device((y + 2) % RING, z, core)

    def con_copy(s):
        return remote(con_out.at[s], con_in.at[s], con_ss.at[s], con_rs.at[s], partner)

    def half_of(part):
        return pl.ds(pl.multiple_of(part * columns, columns), columns)

    def up(s):
        def pair_arrived(pair):
            normed_arrived(2 * pair, s)
            normed_arrived(2 * pair + 1, s)

        normalize(0, s)
        arrived(1, s)
        normalize(1, s)
        if s == 0:
            arrived(4, 1)
            for n in (5, 7, 6):
                block_copy(n, 1).start()
        acc[s] = jnp.zeros(acc.shape[1:], F32)

        def take(pair):
            @pl.when(pair == 3 if s == 0 else pair != 2)
            def _():
                arrived(2 * pair, s)

            normalize(2 * pair, s)
            arrived(2 * pair + 1, s)
            normalize(2 * pair + 1, s)
            pair_arrived(pair - 1)
            acc[s] = acc[s] + jnp.dot(normed[pair - 1, s], w[pair - 1], preferred_element_type=F32)
            if s == 1:
                release(pair - 1)

        loop(1, RING, take)
        last = RING - 1
        pair_arrived(last)
        for part in (1 - con, con):
            term = acc[s, :, half_of(part)] + jnp.dot(
                normed[last, s], w[last, :, half_of(part)], preferred_element_type=F32
            )
            if part is con:
                acc[s, :, half_of(con)] = term
            else:
                con_out[s] = term.astype(BF16)
                con_copy(s).start()
        if s == 1:
            release(last)

    def activate(s):
        con_copy(s).wait_recv()

        def piece(r):
            rows = pl.ds(pl.multiple_of(r * 32, 32), 32)
            v = acc[s, rows, half_of(con)] + con_in[s, rows, :].astype(F32)
            hidden[s, rows, :] = (0.5 * v * (1.0 + lax.erf(v * (0.5**0.5)))).astype(BF16)

        loop(0, half // 32, piece)

    up(0)
    up(1)
    activate(0)
    loop(0, chips, lambda q: w_copy(q).wait())

    def reduce(me):
        bounds = ((0, FIRST), (FIRST, half))
        count = [stop - start for start, stop in bounds]
        rows, other = count[me], count[1 - me]

        def product(role, first, second, s):
            py, pz = shifted(y, z, role, first, second)
            taken = pl.ds(bounds[role][0], count[role])
            return jnp.dot(
                hidden[s, taken, :], down_block(py * RING + pz)[...], preferred_element_type=F32
            )

        def sib_send(t, s):
            taken = pl.ds(0, other)
            return remote(sib_out.at[t, taken], sib_in.at[t, s, taken], sib_ss.at[t, s], sib_rs.at[t, s], sibling)

        def sib_arrived(t, s):
            taken = pl.ds(0, rows)
            remote(
                sib_out.at[t, taken], sib_in.at[t, s, taken], sib_ss.at[t, s], sib_rs.at[t, s], sibling
            ).wait_recv()

        def slot(t, s):
            return t + t // (2 * RING) * 2 * RING * s

        def total(t, s):
            return own[slot(t, s), :rows] + sib_in[t, s, :rows].astype(F32)

        def copy1(kind, j):
            ty, tz = shifted(y, z, me, 1 if kind % 2 == 0 else 3, 0)
            taken = pl.ds(0, rows)
            return remote(
                s1.at[kind, j, taken], r1.at[kind, j, taken], ss1.at[kind, j], rs1.at[kind, j], device(ty, tz, me)
            )

        def copy2(s, j):
            ty, tz = shifted(y, z, me, 0, offset(j))
            taken = pl.ds(0, rows)
            return remote(
                s2.at[s, j, taken], r2.at[s, j, taken], ss2.at[s, j], rs2.at[s, j], device(ty, tz, me)
            )

        def compute(t, s):
            group, second = t // RING, offset(t % RING)
            first = offset(group) if s == 1 else (RING - offset(group)) % RING
            if s == 1:
                sib_send(t, 0).wait_send()
            sib_out[t, :other] = product(1 - me, first, second, s).astype(BF16)
            sib_send(t, s).start()
            own[slot(t, s), :rows] = product(me, first, second, s)

        def send_direct(t, s):
            sib_arrived(t, s)

            @pl.when(t < RING)
            def _():
                s1[s, t, :rows] = total(t, s).astype(BF16)
                copy1(s, t).start()

            @pl.when(t >= RING)
            def _():
                s1[3 - s, t - RING, :rows] = total(t, s).astype(BF16)
                copy1(3 - s, t - RING).start()

        def direct(s):
            compute(0, s)

            def step(t):
                compute(t, s)
                send_direct(t - 1, s)

            loop(1, 2 * RING + 1, step)
            loop(2 * RING + 1, 3 * RING, lambda t: compute(t, s))

        def relay(s):
            def step(j):
                t = 2 * RING + j
                sib_arrived(t, s)
                copy1(s, j).wait_recv()
                s1[4 + s, j, :rows] = (total(t, s) + r1[s, j, :rows].astype(F32)).astype(BF16)
                copy1(4 + s, j).start()

            loop(0, RING, step)

        direct(0)
        activate(1)
        loop(3 * RING, chips, lambda t: compute(t, 0))
        direct(1)
        relay(0)
        loop(3 * RING, chips, lambda t: compute(t, 1))
        relay(1)

        def summed(j, s):
            sib_arrived(3 * RING + j, s)
            copy1(3 - s, j).wait_recv()
            copy1(4 + s, j).wait_recv()
            return total(3 * RING + j, s) + r1[4 + s, j, :rows].astype(F32) + r1[3 - s, j, :rows].astype(F32)

        for s in range(2):
            for j in range(3):
                s2[s, j, :rows] = summed(j, s).astype(BF16)
                copy2(s, j).start()
        if me == 0:
            pieces = [(0, quarter, 0), (quarter, FIRST - quarter, half)]
        else:
            pieces = [(0, half - FIRST, half + FIRST - quarter)]
        final_copies = []
        for s in range(2):
            final = summed(3, s)
            for j in range(3):
                copy2(s, j).wait_recv()
                final = final + r2[s, j, :rows].astype(F32)
            left, right = final[:, : columns // 2], final[:, columns // 2 :]
            kept, given = (left, right) if me == 0 else (right, left)
            fin[s, :rows] = given.astype(BF16)
            for k, (begin, size, token) in enumerate(pieces):
                target = pl.ds(token + s * quarter, size)
                final_copy = remote(
                    fin.at[s, pl.ds(begin, size)], o_ref.at[target], fin_ss.at[s, k], fin_rs.at[me, s, k], sibling
                )
                final_copy.start()
                final_copies.append(final_copy)
                o_ref[target, :] = kept[begin : begin + size].astype(BF16)

        def drain(j):
            for kind in range(6):
                copy1(kind, j).wait_send()
            for group in range(4):
                sib_send(group * RING + j, 1).wait_send()

        loop(0, RING, drain)
        for s in range(2):
            for j in range(3):
                copy2(s, j).wait_send()
        for final_copy in final_copies:
            final_copy.wait_send()
        theirs_pieces = [(0, half - FIRST, half + FIRST - quarter)]
        if me == 1:
            theirs_pieces = [(0, quarter, 0), (quarter, FIRST - quarter, half)]
        for s in range(2):
            for k, (begin, size, token) in enumerate(theirs_pieces):
                target = pl.ds(token + s * quarter, size)
                remote(
                    fin.at[s, pl.ds(begin, size)], o_ref.at[target], fin_ss.at[s, k], fin_rs.at[1 - me, s, k], sibling
                ).wait_recv()

    for me in range(2):
        pl.when(core == me)(functools.partial(reduce, me))
    x_copy.wait_send()
    gain_copy.wait_send()
    loop(1, chips, lambda q: stat_to(q).wait_send())
    for s in range(2):
        for n in range(1, 8):
            block_copy(n, s).wait_send()
        for n in range(8):
            normed_copy(n, s).wait_send()
        con_copy(s).wait_send()


def local(tokens, gain, up_weight, down_weight):
    count, features = tokens.shape
    units, width = down_weight.shape
    chips = RING * RING
    columns = width // chips
    half, quarter, most = count // 2, count // 4, FIRST
    dma = pltpu.SemaphoreType.DMA
    vmem = pl.BlockSpec(memory_space=pltpu.VMEM)
    hbm = pl.BlockSpec(memory_space=pl.ANY)
    return pl.pallas_call(
        block_kernel,
        out_shape=jax.ShapeDtypeStruct((count, columns // 2), BF16),
        in_specs=[hbm, vmem, hbm, hbm],
        out_specs=vmem,
        scratch_shapes=[
            pltpu.VMEM((features, count), BF16),
            pltpu.VMEM((RING, 2 * columns, 2 * columns), BF16),
            pltpu.VMEM((2, columns, 2, units), BF16),
            pltpu.VMEM((features, half), BF16),
            pltpu.VMEM((columns, half), BF16),
            pltpu.VMEM((8, features), F32),
            pltpu.VMEM((8, features), F32),
            pltpu.VMEM((16, 128), F32),
            pltpu.VMEM((chips, 16, 128), F32),
            pltpu.VMEM((8, half, columns), BF16),
            pltpu.VMEM((RING, 2, half, 2 * columns), BF16),
            pltpu.VMEM((2, half, 128), F32),
            pltpu.VMEM((2, half, 2 * units), F32),
            pltpu.VMEM((2, half, units), BF16),
            pltpu.VMEM((2, half, units), BF16),
            pltpu.VMEM((2, half, units), BF16),
            pltpu.VMEM((6 * RING, most, columns), F32),
            pltpu.VMEM((chips, most, columns), BF16),
            pltpu.VMEM((chips, 2, most, columns), BF16),
            pltpu.VMEM((6, RING, most, columns), BF16),
            pltpu.VMEM((6, RING, most, columns), BF16),
            pltpu.VMEM((2, 3, most, columns), BF16),
            pltpu.VMEM((2, 3, most, columns), BF16),
            pltpu.VMEM((2, most, columns // 2), BF16),
            dma, dma((chips,)), dma((2,)), dma, dma, dma, dma, dma((chips,)), dma((chips,)),
            dma((8, 2)), dma((8, 2)), dma((8, 2)), dma((8, 2)), dma((2,)), dma((2,)),
            dma((chips, 2)), dma((chips, 2)), dma((6, RING)), dma((6, RING)), dma((2, 3)), dma((2, 3)), dma((2, 2)), dma((2, 2, 2)),
        ],
        name="block",
        compiler_params=pltpu.CompilerParams(
            collective_id=1, has_side_effects=True, vmem_limit_bytes=62 << 20
        ),
    )(tokens.T, gain, up_weight, down_weight)


def solution(mesh):
    in_specs = (
        P("tok", ("con", "out")),
        P(("con", "out")),
        P("con", None, "out"),
        P(("con", "out"), None),
    )
    out_specs = P("tok", ("con", "out"))
    return jax.shard_map(local, mesh=mesh, in_specs=in_specs, out_specs=out_specs, check_vma=False)
```

```python
import functools

import jax
import jax.numpy as jnp
from jax import lax
from jax.experimental import pallas as pl
from jax.experimental.pallas import tpu as pltpu
from jax.sharding import PartitionSpec as P

D = 10240
RING = 4
MESH = pl.DeviceIdType.MESH
F32, BF16 = jnp.float32, jnp.bfloat16


def place():
    con, out = lax.axis_index("con"), lax.axis_index("out")
    return con * 2 + out // 8, (out // 2) % RING, out % 2


def device(y, z, core):
    return (lax.axis_index("tok"), y // 2, (y % 2) * 8 + z * 2 + core)


def shifted(y, z, role, first, second):
    return (
        (y + first * role + second * (1 - role)) % RING,
        (z + first * (1 - role) + second * role) % RING,
    )


def offset(j):
    swapped = j + (j // 2) * (5 - 2 * j)
    return (2 - swapped + RING) % RING


def loop(start, stop, body):
    def step(i, carry):
        body(i)
        return carry

    lax.fori_loop(start, stop, step, 0)


def block_kernel(
    xt_hbm, gain_ref, u_hbm, w_hbm, o_ref,
    xt_ref, w, raw, sib_xt, tall, own_gain, sib_gain, stat_out, stat_in, blocks, normed, columns_of,
    acc, con_out, con_in, hidden, own, sib_out, sib_in, s1, r1, s2, r2, fin,
    xt_sem, w_sem, raw_sem, sx_ss, sx_rs, sg_ss, sg_rs, st_ss, st_rs, bl_ss, bl_rs, nm_ss, nm_rs, con_ss, con_rs,
    sib_ss, sib_rs, ss1, rs1, ss2, rs2, fin_ss, fin_rs,
):
    y, z, core = place()
    con, low = y // 2, y % 2
    features, tokens = xt_ref.shape
    half = tokens // 2
    quarter = half // 2
    columns = s2.shape[-1]
    chips = RING * RING
    sibling = device(y, z, 1 - core)
    mine = pl.ds(pl.multiple_of(core * half, half), half)
    theirs = pl.ds(pl.multiple_of((1 - core) * half, half), half)
    my_quarter = pl.ds(pl.multiple_of(core * quarter, quarter), quarter)

    def remote(source, target, send, recv, where):
        return pltpu.make_async_remote_copy(
            source, target, send, recv, device_id=where, device_id_type=MESH
        )

    def raw_copy(b):
        rows = pl.ds(pl.multiple_of(b * columns, columns), columns)
        return pltpu.make_async_copy(u_hbm.at[rows], raw.at[b % 2], raw_sem.at[b % 2])

    xt_copy = pltpu.make_async_copy(xt_hbm, xt_ref, xt_sem)
    xt_copy.start()
    raw_copy(0).start()
    barrier = pltpu.get_barrier_semaphore()
    pl.semaphore_signal(barrier, inc=1, device_id=sibling, device_id_type=MESH)

    def chip_at(q):
        return device((y + q // RING) % RING, (z + q) % RING, core)

    def greet(q):
        pl.semaphore_signal(barrier, inc=1, device_id=chip_at(q), device_id_type=MESH)

    loop(1, chips, greet)

    gain = gain_ref[...].astype(F32).reshape(1, features)
    own_gain[...] = jnp.broadcast_to(gain, (8, features))
    xt_copy.wait()
    tall[pl.ds(pl.multiple_of(core * features, features), features), :] = xt_ref[:, mine]
    stat_out[...] = jnp.zeros(stat_out.shape, F32)
    pl.semaphore_wait(barrier, chips)
    x_copy = remote(xt_ref.at[:, theirs], sib_xt, sx_ss, sx_rs, sibling)
    x_copy.start()
    gain_copy = remote(own_gain, sib_gain, sg_ss, sg_rs, sibling)
    gain_copy.start()
    x_copy.wait_recv()
    tall[pl.ds(pl.multiple_of((1 - core) * features, features), features), :] = sib_xt[...]
    for c in range(columns // 128):
        lanes = slice(c * 128, (c + 1) * 128)
        blocks[0, :, lanes] = tall[lanes, :].T

    routes = {4: (0, 1, 0), 1: (0, 0, 3), 3: (0, 0, 1), 2: (0, 0, 2), 5: (4, 0, 3), 7: (4, 0, 1)}

    def block_copy(n, s):
        source, dy, dz = routes[n] if n != 6 else ((2, 1, 0), (4, 0, 2))[s]
        rows = pl.ds(s * quarter, quarter)
        where = device(con * 2 + (low + dy) % 2, (z + dz) % RING, core)
        return remote(
            blocks.at[source, rows], blocks.at[n, rows], bl_ss.at[n, s], bl_rs.at[n, s], where
        )

    def arrived(n, s):
        rows = pl.ds(s * quarter, quarter)
        remote(
            blocks.at[0, rows], blocks.at[n, rows], bl_ss.at[n, s], bl_rs.at[n, s], sibling
        ).wait_recv()

    for n in (4, 1, 3, 2):
        block_copy(n, 0).start()

    values = tall[...].astype(F32)
    sums = jnp.sum(values, axis=0, keepdims=True)
    squares = jnp.sum(values * values, axis=0, keepdims=True)
    gain_copy.wait_recv()
    first = core == 0
    other_gain = sib_gain[0:1, :]
    chip_gain = jnp.concatenate(
        [jnp.where(first, gain, other_gain), jnp.where(first, other_gain, gain)], axis=1
    )
    for k in range(half // 128):
        lanes = slice(k * 128, (k + 1) * 128)
        stat_out[k : k + 1, :] = sums[:, lanes]
        stat_out[2 + k : 3 + k, :] = squares[:, lanes]
    for k in range(columns // 128):
        stat_out[8 + k : 9 + k, :] = chip_gain[:, k * 128 : (k + 1) * 128]

    def stat_to(q):
        where = device((y + RING - q // RING) % RING, (z + chips - q) % RING, core)
        return remote(stat_out, stat_in.at[q], st_ss.at[q], st_rs.at[q], where)

    loop(1, chips, lambda q: stat_to(q).start())

    def unpack(b):
        @pl.when(b + 1 < 8)
        def _():
            raw_copy(b + 1).start()

        raw_copy(b).wait()

        def piece(r):
            rows = pl.ds(pl.multiple_of(r * 64, 64), 64)
            both = pltpu.einshape("khn->hkn", raw[b % 2, rows])
            w[2 * b, rows, :] = both[0]
            w[2 * b + 1, rows, :] = both[1]

        loop(0, columns // 64, piece)

    loop(0, 2, unpack)
    arrived(4, 0)
    block_copy(5, 0).start()
    block_copy(7, 0).start()
    for n in (4, 1, 3, 2):
        block_copy(n, 1).start()
    loop(2, 5, unpack)
    arrived(2, 0)
    block_copy(6, 0).start()
    loop(5, 8, unpack)

    stat_in[0] = stat_out[...]
    loop(1, chips, lambda q: stat_to(q).wait_recv())
    whole = stat_in[0]
    for q in range(1, chips):
        whole = whole + stat_in[q]
    average = whole[0:2, :] / D
    scale = lax.rsqrt(whole[2:4, :] / D - average * average + 1e-05)
    for k in range(2):
        rows = slice(k * 128, (k + 1) * 128)
        columns_of[0, rows, :] = jnp.broadcast_to(average[k : k + 1, :], (128, 128)).T
        columns_of[1, rows, :] = jnp.broadcast_to(scale[k : k + 1, :], (128, 128)).T

    def weight_of(n):
        return (low + n // RING) % 2 * RING + (z + n) % RING

    def normed_copy(n, s):
        return remote(
            normed.at[n, s, my_quarter], normed.at[n, s, my_quarter], nm_ss.at[n, s], nm_rs.at[n, s], sibling
        )

    def normed_arrived(n, s):
        rows = pl.ds(pl.multiple_of((1 - core) * quarter, quarter), quarter)
        remote(
            normed.at[n, s, rows], normed.at[n, s, rows], nm_ss.at[n, s], nm_rs.at[n, s], sibling
        ).wait_recv()

    def normalize(n, s):
        seen = (n // RING * (1 - 2 * low) + RING) % RING * RING + n % RING
        gains = jnp.concatenate(
            [stat_in[seen, 8 + k : 9 + k, :] for k in range(columns // 128)], axis=1
        )

        def piece(r):
            rows = pl.ds(pl.multiple_of(s * quarter + r * 32, 32), 32)
            shape = (1, columns // 128)
            average = jnp.tile(columns_of[0, rows, :], shape)
            scale = jnp.tile(columns_of[1, rows, :], shape)
            values = blocks[n, rows, :].astype(F32)
            place_to = pl.ds(pl.multiple_of(core * quarter + r * 32, 32), 32)
            normed[n, s, place_to, :] = ((values - average) * scale * gains).astype(BF16)

        loop(0, quarter // 32, piece)
        normed_copy(n, s).start()

    def w_copy(q):
        cols = pl.ds(pl.multiple_of(q * columns, columns), columns)
        return pltpu.make_async_copy(w_hbm.at[:, cols], w.at[q], w_sem.at[q])

    def release(n):
        for part in range(2):
            w_copy(2 * weight_of(n) + part).start()

    def update(n, s, part, start=False):
        term = jnp.dot(normed[n, s], w[2 * weight_of(n) + part], preferred_element_type=F32)
        acc[part, s] = term if start else acc[part, s] + term

    partner = device((y + 2) % RING, z, core)

    def con_copy(s):
        return remote(con_out.at[s], con_in.at[s], con_ss.at[s], con_rs.at[s], partner)

    def up(s):
        normalize(0, s)
        arrived(1, s)
        if s == 0:
            arrived(4, 1)
            for n in (5, 7, 6):
                block_copy(n, 1).start()
        normalize(1, s)
        normed_arrived(0, s)
        for part in range(2):
            update(0, s, part, True)
        if s == 1:
            release(0)

        def take(n):
            @pl.when((n != 4) & ((n != 2) | (s == 1)))
            def _():
                arrived(n, s)

            normalize(n, s)
            normed_arrived(n - 1, s)
            for part in range(2):
                update(n - 1, s, part)
            if s == 1:
                release(n - 1)

        loop(2, 8, take)
        normed_arrived(7, s)
        term = jnp.dot(normed[7, s], w[2 * weight_of(7) + 1 - con], preferred_element_type=F32)
        con_out[s] = (acc[1 - con, s] + term).astype(BF16)
        con_copy(s).start()
        update(7, s, con)
        if s == 1:
            release(7)

    def activate(s):
        con_copy(s).wait_recv()

        def piece(r):
            rows = pl.ds(pl.multiple_of(r * 32, 32), 32)
            v = acc[con, s, rows, :] + con_in[s, rows, :].astype(F32)
            hidden[s, rows, :] = (0.5 * v * (1.0 + lax.erf(v * (0.5**0.5)))).astype(BF16)

        loop(0, half // 32, piece)

    def product(role, first, second, s):
        py, pz = shifted(y, z, role, first, second)
        rows = pl.ds(pl.multiple_of(role * quarter, quarter), quarter)
        return jnp.dot(hidden[s, rows, :], w[py * RING + pz], preferred_element_type=F32)

    def sib_copy(t, s):
        return remote(sib_out.at[t, s], sib_in.at[t, s], sib_ss.at[t, s], sib_rs.at[t, s], sibling)

    def slot(t, s):
        return t + t // (2 * RING) * 2 * RING * s

    def total(t, s):
        return own[slot(t, s)] + sib_in[t, s].astype(F32)

    def copy1(kind, j):
        ty, tz = shifted(y, z, core, 1 if kind % 2 == 0 else 3, 0)
        return remote(s1.at[kind, j], r1.at[kind, j], ss1.at[kind, j], rs1.at[kind, j], device(ty, tz, core))

    def copy2(s, j):
        ty, tz = shifted(y, z, core, 0, offset(j))
        return remote(s2.at[s, j], r2.at[s, j], ss2.at[s, j], rs2.at[s, j], device(ty, tz, core))

    def compute(t, s):
        group, second = t // RING, offset(t % RING)
        first = offset(group) if s == 1 else (RING - offset(group)) % RING
        sib_out[t, s] = product(1 - core, first, second, s).astype(BF16)
        sib_copy(t, s).start()
        own[slot(t, s)] = product(core, first, second, s)

    def send_direct(t, s):
        sib_copy(t, s).wait_recv()

        @pl.when(t < RING)
        def _():
            s1[s, t] = total(t, s).astype(BF16)
            copy1(s, t).start()

        @pl.when(t >= RING)
        def _():
            s1[3 - s, t - RING] = total(t, s).astype(BF16)
            copy1(3 - s, t - RING).start()

    def direct(s):
        compute(0, s)

        def step(t):
            compute(t, s)
            send_direct(t - 1, s)

        loop(1, 2 * RING, step)
        compute(2 * RING, s)
        send_direct(2 * RING - 1, s)

    def relay(s):
        def step(j):
            t = 2 * RING + j
            sib_copy(t, s).wait_recv()
            copy1(s, j).wait_recv()
            s1[4 + s, j] = (total(t, s) + r1[s, j].astype(F32)).astype(BF16)
            copy1(4 + s, j).start()

        loop(0, RING, step)

    up(0)
    up(1)
    activate(0)
    loop(0, chips, lambda q: w_copy(q).wait())
    direct(0)
    loop(2 * RING + 1, 3 * RING, lambda t: compute(t, 0))
    activate(1)
    direct(1)
    relay(0)
    loop(2 * RING + 1, 3 * RING, lambda t: compute(t, 1))
    loop(3 * RING, chips, lambda t: compute(t, 0))
    loop(3 * RING, chips, lambda t: compute(t, 1))
    relay(1)

    def summed(j, s):
        sib_copy(3 * RING + j, s).wait_recv()
        copy1(3 - s, j).wait_recv()
        copy1(4 + s, j).wait_recv()
        return total(3 * RING + j, s) + r1[4 + s, j].astype(F32) + r1[3 - s, j].astype(F32)

    for s in range(2):
        for j in range(3):
            s2[s, j] = summed(j, s).astype(BF16)
            copy2(s, j).start()
    final_copies = []
    for s in range(2):
        final = summed(3, s)
        for j in range(3):
            copy2(s, j).wait_recv()
            final = final + r2[s, j].astype(F32)
        final = final.T
        left, right = final[: columns // 2], final[columns // 2 :]
        fin[s] = jnp.where(core == 0, right, left).astype(BF16)
        rows = pl.ds(pl.multiple_of(core * half + s * quarter, quarter), quarter)
        final_copy = remote(fin.at[s], o_ref.at[:, rows], fin_ss.at[s], fin_rs.at[s], sibling)
        final_copy.start()
        final_copies.append(final_copy)
        o_ref[:, rows] = jnp.where(core == 0, left, right).astype(BF16)

    def drain(j):
        for kind in range(6):
            copy1(kind, j).wait_send()
        for group in range(4):
            for s in range(2):
                sib_copy(group * RING + j, s).wait_send()

    loop(0, RING, drain)
    for s in range(2):
        for j in range(3):
            copy2(s, j).wait_send()
        final_copies[s].wait()
    x_copy.wait_send()
    gain_copy.wait_send()
    loop(1, chips, lambda q: stat_to(q).wait_send())
    for s in range(2):
        for n in range(1, 8):
            block_copy(n, s).wait_send()
        for n in range(8):
            normed_copy(n, s).wait_send()
        con_copy(s).wait_send()


def local(tokens, gain, up_weight, down_weight):
    count, features = tokens.shape
    units, width = down_weight.shape
    chips = RING * RING
    columns = width // chips
    half, quarter = count // 2, count // 4
    dma = pltpu.SemaphoreType.DMA
    vmem = pl.BlockSpec(memory_space=pltpu.VMEM)
    hbm = pl.BlockSpec(memory_space=pl.ANY)
    return pl.pallas_call(
        block_kernel,
        out_shape=jax.ShapeDtypeStruct((columns // 2, count), BF16),
        in_specs=[hbm, vmem, hbm, hbm],
        out_specs=vmem,
        scratch_shapes=[
            pltpu.VMEM((features, count), BF16),
            pltpu.VMEM((chips, columns, columns), BF16),
            pltpu.VMEM((2, columns, 2, units), BF16),
            pltpu.VMEM((features, half), BF16),
            pltpu.VMEM((columns, half), BF16),
            pltpu.VMEM((8, features), F32),
            pltpu.VMEM((8, features), F32),
            pltpu.VMEM((16, 128), F32),
            pltpu.VMEM((chips, 16, 128), F32),
            pltpu.VMEM((8, half, columns), BF16),
            pltpu.VMEM((8, 2, half, columns), BF16),
            pltpu.VMEM((2, half, 128), F32),
            pltpu.VMEM((2, 2, half, units), F32),
            pltpu.VMEM((2, half, units), BF16),
            pltpu.VMEM((2, half, units), BF16),
            pltpu.VMEM((2, half, units), BF16),
            pltpu.VMEM((6 * RING, quarter, columns), F32),
            pltpu.VMEM((chips, 2, quarter, columns), BF16),
            pltpu.VMEM((chips, 2, quarter, columns), BF16),
            pltpu.VMEM((6, RING, quarter, columns), BF16),
            pltpu.VMEM((6, RING, quarter, columns), BF16),
            pltpu.VMEM((2, 3, quarter, columns), BF16),
            pltpu.VMEM((2, 3, quarter, columns), BF16),
            pltpu.VMEM((2, columns // 2, quarter), BF16),
            dma, dma((chips,)), dma((2,)), dma, dma, dma, dma, dma((chips,)), dma((chips,)),
            dma((8, 2)), dma((8, 2)), dma((8, 2)), dma((8, 2)), dma((2,)), dma((2,)),
            dma((chips, 2)), dma((chips, 2)), dma((6, RING)), dma((6, RING)), dma((2, 3)), dma((2, 3)), dma((2,)), dma((2,)),
        ],
        name="block",
        compiler_params=pltpu.CompilerParams(
            collective_id=1, has_side_effects=True, vmem_limit_bytes=62 << 20
        ),
    )(tokens.T, gain, up_weight, down_weight).T


def solution(mesh):
    in_specs = (
        P("tok", ("con", "out")),
        P(("con", "out")),
        P("con", None, "out"),
        P(("con", "out"), None),
    )
    out_specs = P("tok", ("con", "out"))
    return jax.shard_map(local, mesh=mesh, in_specs=in_specs, out_specs=out_specs, check_vma=False)
```

```python
import functools

import jax
import jax.numpy as jnp
from jax import lax
from jax.experimental import pallas as pl
from jax.experimental.pallas import tpu as pltpu
from jax.sharding import PartitionSpec as P

D = 10240
RING = 4
MESH = pl.DeviceIdType.MESH
F32, BF16 = jnp.float32, jnp.bfloat16


def place():
    con, out = lax.axis_index("con"), lax.axis_index("out")
    return con * 2 + out // 8, (out // 2) % RING, out % 2


def device(y, z, core):
    return (lax.axis_index("tok"), y // 2, (y % 2) * 8 + z * 2 + core)


def shifted(y, z, role, first, second):
    return (
        (y + first * role + second * (1 - role)) % RING,
        (z + first * (1 - role) + second * role) % RING,
    )


def offset(j):
    swapped = j + (j // 2) * (5 - 2 * j)
    return (2 - swapped + RING) % RING


def loop(start, stop, body):
    def step(i, carry):
        body(i)
        return carry

    lax.fori_loop(start, stop, step, 0)


def block_kernel(
    xt_hbm, gain_ref, u_hbm, w_hbm, o_ref,
    xt_ref, w, raw, sib_xt, tall, own_gain, sib_gain, stat_out, stat_in, blocks, normed, columns_of,
    acc, con_out, con_in, hidden, own, sib_out, sib_in, s1, r1, s2, r2, fin,
    xt_sem, w_sem, raw_sem, sx_ss, sx_rs, sg_ss, sg_rs, st_ss, st_rs, bl_ss, bl_rs, nm_ss, nm_rs, con_ss, con_rs,
    sib_ss, sib_rs, ss1, rs1, ss2, rs2, fin_ss, fin_rs,
):
    y, z, core = place()
    con, low = y // 2, y % 2
    features, tokens = xt_ref.shape
    half = tokens // 2
    quarter = half // 2
    columns = s2.shape[-1]
    chips = RING * RING
    sibling = device(y, z, 1 - core)
    mine = pl.ds(pl.multiple_of(core * half, half), half)
    theirs = pl.ds(pl.multiple_of((1 - core) * half, half), half)
    my_quarter = pl.ds(pl.multiple_of(core * quarter, quarter), quarter)

    def remote(source, target, send, recv, where):
        return pltpu.make_async_remote_copy(
            source, target, send, recv, device_id=where, device_id_type=MESH
        )

    def raw_copy(b):
        rows = pl.ds(pl.multiple_of(b * columns, columns), columns)
        return pltpu.make_async_copy(u_hbm.at[rows], raw.at[b % 2], raw_sem.at[b % 2])

    xt_copy = pltpu.make_async_copy(xt_hbm, xt_ref, xt_sem)
    xt_copy.start()
    raw_copy(0).start()
    barrier = pltpu.get_barrier_semaphore()
    pl.semaphore_signal(barrier, inc=1, device_id=sibling, device_id_type=MESH)

    def chip_at(q):
        return device((y + q // RING) % RING, (z + q) % RING, core)

    def greet(q):
        pl.semaphore_signal(barrier, inc=1, device_id=chip_at(q), device_id_type=MESH)

    loop(1, chips, greet)

    gain = gain_ref[...].astype(F32).reshape(1, features)
    own_gain[...] = jnp.broadcast_to(gain, (8, features))
    xt_copy.wait()
    tall[pl.ds(pl.multiple_of(core * features, features), features), :] = xt_ref[:, mine]
    stat_out[...] = jnp.zeros(stat_out.shape, F32)
    pl.semaphore_wait(barrier, chips)
    x_copy = remote(xt_ref.at[:, theirs], sib_xt, sx_ss, sx_rs, sibling)
    x_copy.start()
    gain_copy = remote(own_gain, sib_gain, sg_ss, sg_rs, sibling)
    gain_copy.start()
    x_copy.wait_recv()
    tall[pl.ds(pl.multiple_of((1 - core) * features, features), features), :] = sib_xt[...]
    for c in range(columns // 128):
        lanes = slice(c * 128, (c + 1) * 128)
        blocks[0, :, lanes] = tall[lanes, :].T

    routes = {4: (0, 1, 0), 1: (0, 0, 3), 3: (0, 0, 1), 2: (0, 0, 2), 5: (4, 0, 3), 7: (4, 0, 1)}

    def block_copy(n, s):
        source, dy, dz = routes[n] if n != 6 else ((2, 1, 0), (4, 0, 2))[s]
        rows = pl.ds(s * quarter, quarter)
        where = device(con * 2 + (low + dy) % 2, (z + dz) % RING, core)
        return remote(
            blocks.at[source, rows], blocks.at[n, rows], bl_ss.at[n, s], bl_rs.at[n, s], where
        )

    def arrived(n, s):
        rows = pl.ds(s * quarter, quarter)
        remote(
            blocks.at[0, rows], blocks.at[n, rows], bl_ss.at[n, s], bl_rs.at[n, s], sibling
        ).wait_recv()

    for n in (4, 2, 1, 3):
        block_copy(n, 0).start()

    values = tall[...].astype(F32)
    sums = jnp.sum(values, axis=0, keepdims=True)
    squares = jnp.sum(values * values, axis=0, keepdims=True)
    gain_copy.wait_recv()
    first = core == 0
    other_gain = sib_gain[0:1, :]
    chip_gain = jnp.concatenate(
        [jnp.where(first, gain, other_gain), jnp.where(first, other_gain, gain)], axis=1
    )
    for k in range(half // 128):
        lanes = slice(k * 128, (k + 1) * 128)
        stat_out[k : k + 1, :] = sums[:, lanes]
        stat_out[2 + k : 3 + k, :] = squares[:, lanes]
    for k in range(columns // 128):
        stat_out[8 + k : 9 + k, :] = chip_gain[:, k * 128 : (k + 1) * 128]

    def stat_to(q):
        where = device((y + RING - q // RING) % RING, (z + chips - q) % RING, core)
        return remote(stat_out, stat_in.at[q], st_ss.at[q], st_rs.at[q], where)

    loop(1, chips, lambda q: stat_to(q).start())

    def unpack(b):
        @pl.when(b + 1 < 8)
        def _():
            raw_copy(b + 1).start()

        raw_copy(b).wait()

        def piece(r):
            rows = pl.ds(pl.multiple_of(r * 64, 64), 64)
            both = pltpu.einshape("khn->hkn", raw[b % 2, rows])
            w[2 * b, rows, :] = both[0]
            w[2 * b + 1, rows, :] = both[1]

        loop(0, columns // 64, piece)

    loop(0, 2, unpack)
    arrived(4, 0)
    block_copy(5, 0).start()
    block_copy(7, 0).start()
    for n in (4, 2, 1, 3):
        block_copy(n, 1).start()
    loop(2, 5, unpack)
    arrived(2, 0)
    block_copy(6, 0).start()
    loop(5, 8, unpack)

    stat_in[0] = stat_out[...]
    loop(1, chips, lambda q: stat_to(q).wait_recv())
    whole = stat_in[0]
    for q in range(1, chips):
        whole = whole + stat_in[q]
    average = whole[0:2, :] / D
    scale = lax.rsqrt(whole[2:4, :] / D - average * average + 1e-05)
    for k in range(2):
        rows = slice(k * 128, (k + 1) * 128)
        columns_of[0, rows, :] = jnp.broadcast_to(average[k : k + 1, :], (128, 128)).T
        columns_of[1, rows, :] = jnp.broadcast_to(scale[k : k + 1, :], (128, 128)).T

    def weight_of(n):
        return (low + n // RING) % 2 * RING + (z + n) % RING

    def normed_copy(n, s):
        return remote(
            normed.at[n, s, my_quarter], normed.at[n, s, my_quarter], nm_ss.at[n, s], nm_rs.at[n, s], sibling
        )

    def normed_arrived(n, s):
        rows = pl.ds(pl.multiple_of((1 - core) * quarter, quarter), quarter)
        remote(
            normed.at[n, s, rows], normed.at[n, s, rows], nm_ss.at[n, s], nm_rs.at[n, s], sibling
        ).wait_recv()

    def normalize(n, s):
        seen = (n // RING * (1 - 2 * low) + RING) % RING * RING + n % RING
        gains = jnp.concatenate(
            [stat_in[seen, 8 + k : 9 + k, :] for k in range(columns // 128)], axis=1
        )

        def piece(r):
            rows = pl.ds(pl.multiple_of(s * quarter + r * 32, 32), 32)
            shape = (1, columns // 128)
            average = jnp.tile(columns_of[0, rows, :], shape)
            scale = jnp.tile(columns_of[1, rows, :], shape)
            values = blocks[n, rows, :].astype(F32)
            place_to = pl.ds(pl.multiple_of(core * quarter + r * 32, 32), 32)
            normed[n, s, place_to, :] = ((values - average) * scale * gains).astype(BF16)

        loop(0, quarter // 32, piece)
        normed_copy(n, s).start()

    def w_copy(q):
        cols = pl.ds(pl.multiple_of(q * columns, columns), columns)
        return pltpu.make_async_copy(w_hbm.at[:, cols], w.at[q], w_sem.at[q])

    def release(n):
        for part in range(2):
            w_copy(2 * weight_of(n) + part).start()

    def update(n, s, part, start=False):
        term = jnp.dot(normed[n, s], w[2 * weight_of(n) + part], preferred_element_type=F32)
        acc[part, s] = term if start else acc[part, s] + term

    partner = device((y + 2) % RING, z, core)

    def con_copy(s):
        return remote(con_out.at[s], con_in.at[s], con_ss.at[s], con_rs.at[s], partner)

    def up(s):
        normalize(0, s)
        arrived(1, s)
        if s == 0:
            arrived(4, 1)
            for n in (5, 7, 6):
                block_copy(n, 1).start()
        normalize(1, s)
        normed_arrived(0, s)
        for part in range(2):
            update(0, s, part, True)
        if s == 1:
            release(0)

        def take(n):
            @pl.when((n != 4) & ((n != 2) | (s == 1)))
            def _():
                arrived(n, s)

            normalize(n, s)
            normed_arrived(n - 1, s)
            for part in range(2):
                update(n - 1, s, part)
            if s == 1:
                release(n - 1)

        loop(2, 8, take)
        normed_arrived(7, s)
        term = jnp.dot(normed[7, s], w[2 * weight_of(7) + 1 - con], preferred_element_type=F32)
        con_out[s] = (acc[1 - con, s] + term).astype(BF16)
        con_copy(s).start()
        update(7, s, con)
        if s == 1:
            release(7)

    def activate(s):
        con_copy(s).wait_recv()

        def piece(r):
            rows = pl.ds(pl.multiple_of(r * 32, 32), 32)
            v = acc[con, s, rows, :] + con_in[s, rows, :].astype(F32)
            hidden[s, rows, :] = (0.5 * v * (1.0 + lax.erf(v * (0.5**0.5)))).astype(BF16)

        loop(0, half // 32, piece)

    def product(role, first, second, s):
        py, pz = shifted(y, z, role, first, second)
        rows = pl.ds(pl.multiple_of(role * quarter, quarter), quarter)
        return jnp.dot(hidden[s, rows, :], w[py * RING + pz], preferred_element_type=F32)

    def sib_copy(t, s):
        return remote(sib_out.at[t, s], sib_in.at[t, s], sib_ss.at[t, s], sib_rs.at[t, s], sibling)

    def slot(t, s):
        return t + t // (2 * RING) * 2 * RING * s

    def total(t, s):
        return own[slot(t, s)] + sib_in[t, s].astype(F32)

    def copy1(kind, j):
        ty, tz = shifted(y, z, core, 1 if kind % 2 == 0 else 3, 0)
        return remote(s1.at[kind, j], r1.at[kind, j], ss1.at[kind, j], rs1.at[kind, j], device(ty, tz, core))

    def copy2(s, j):
        ty, tz = shifted(y, z, core, 0, offset(j))
        return remote(s2.at[s, j], r2.at[s, j], ss2.at[s, j], rs2.at[s, j], device(ty, tz, core))

    def compute(t, s):
        group, second = t // RING, offset(t % RING)
        first = offset(group) if s == 1 else (RING - offset(group)) % RING
        sib_out[t, s] = product(1 - core, first, second, s).astype(BF16)
        sib_copy(t, s).start()
        own[slot(t, s)] = product(core, first, second, s)

    def send_direct(t, s):
        sib_copy(t, s).wait_recv()

        @pl.when(t < RING)
        def _():
            s1[s, t] = total(t, s).astype(BF16)
            copy1(s, t).start()

        @pl.when(t >= RING)
        def _():
            s1[3 - s, t - RING] = total(t, s).astype(BF16)
            copy1(3 - s, t - RING).start()

    def direct(s):
        compute(0, s)

        def step(t):
            compute(t, s)
            send_direct(t - 1, s)

        loop(1, 2 * RING, step)
        compute(2 * RING, s)
        send_direct(2 * RING - 1, s)

    def relay(s):
        def step(j):
            t = 2 * RING + j
            sib_copy(t, s).wait_recv()
            copy1(s, j).wait_recv()
            s1[4 + s, j] = (total(t, s) + r1[s, j].astype(F32)).astype(BF16)
            copy1(4 + s, j).start()

        loop(0, RING, step)

    up(0)
    up(1)
    activate(0)
    loop(0, chips, lambda q: w_copy(q).wait())
    direct(0)
    loop(2 * RING + 1, 3 * RING, lambda t: compute(t, 0))
    activate(1)
    direct(1)
    relay(0)
    loop(2 * RING + 1, 3 * RING, lambda t: compute(t, 1))
    loop(3 * RING, chips, lambda t: compute(t, 0))
    loop(3 * RING, chips, lambda t: compute(t, 1))
    relay(1)

    def summed(j, s):
        sib_copy(3 * RING + j, s).wait_recv()
        copy1(3 - s, j).wait_recv()
        copy1(4 + s, j).wait_recv()
        return total(3 * RING + j, s) + r1[4 + s, j].astype(F32) + r1[3 - s, j].astype(F32)

    for s in range(2):
        for j in range(3):
            s2[s, j] = summed(j, s).astype(BF16)
            copy2(s, j).start()
    final_copies = []
    for s in range(2):
        final = summed(3, s)
        for j in range(3):
            copy2(s, j).wait_recv()
            final = final + r2[s, j].astype(F32)
        final = final.T
        left, right = final[: columns // 2], final[columns // 2 :]
        fin[s] = jnp.where(core == 0, right, left).astype(BF16)
        rows = pl.ds(pl.multiple_of(core * half + s * quarter, quarter), quarter)
        final_copy = remote(fin.at[s], o_ref.at[:, rows], fin_ss.at[s], fin_rs.at[s], sibling)
        final_copy.start()
        final_copies.append(final_copy)
        o_ref[:, rows] = jnp.where(core == 0, left, right).astype(BF16)

    def drain(j):
        for kind in range(6):
            copy1(kind, j).wait_send()
        for group in range(4):
            for s in range(2):
                sib_copy(group * RING + j, s).wait_send()

    loop(0, RING, drain)
    for s in range(2):
        for j in range(3):
            copy2(s, j).wait_send()
        final_copies[s].wait()
    x_copy.wait_send()
    gain_copy.wait_send()
    loop(1, chips, lambda q: stat_to(q).wait_send())
    for s in range(2):
        for n in range(1, 8):
            block_copy(n, s).wait_send()
        for n in range(8):
            normed_copy(n, s).wait_send()
        con_copy(s).wait_send()


def local(tokens, gain, up_weight, down_weight):
    count, features = tokens.shape
    units, width = down_weight.shape
    chips = RING * RING
    columns = width // chips
    half, quarter = count // 2, count // 4
    dma = pltpu.SemaphoreType.DMA
    vmem = pl.BlockSpec(memory_space=pltpu.VMEM)
    hbm = pl.BlockSpec(memory_space=pl.ANY)
    return pl.pallas_call(
        block_kernel,
        out_shape=jax.ShapeDtypeStruct((columns // 2, count), BF16),
        in_specs=[hbm, vmem, hbm, hbm],
        out_specs=vmem,
        scratch_shapes=[
            pltpu.VMEM((features, count), BF16),
            pltpu.VMEM((chips, columns, columns), BF16),
            pltpu.VMEM((2, columns, 2, units), BF16),
            pltpu.VMEM((features, half), BF16),
            pltpu.VMEM((columns, half), BF16),
            pltpu.VMEM((8, features), F32),
            pltpu.VMEM((8, features), F32),
            pltpu.VMEM((16, 128), F32),
            pltpu.VMEM((chips, 16, 128), F32),
            pltpu.VMEM((8, half, columns), BF16),
            pltpu.VMEM((8, 2, half, columns), BF16),
            pltpu.VMEM((2, half, 128), F32),
            pltpu.VMEM((2, 2, half, units), F32),
            pltpu.VMEM((2, half, units), BF16),
            pltpu.VMEM((2, half, units), BF16),
            pltpu.VMEM((2, half, units), BF16),
            pltpu.VMEM((6 * RING, quarter, columns), F32),
            pltpu.VMEM((chips, 2, quarter, columns), BF16),
            pltpu.VMEM((chips, 2, quarter, columns), BF16),
            pltpu.VMEM((6, RING, quarter, columns), BF16),
            pltpu.VMEM((6, RING, quarter, columns), BF16),
            pltpu.VMEM((2, 3, quarter, columns), BF16),
            pltpu.VMEM((2, 3, quarter, columns), BF16),
            pltpu.VMEM((2, columns // 2, quarter), BF16),
            dma, dma((chips,)), dma((2,)), dma, dma, dma, dma, dma((chips,)), dma((chips,)),
            dma((8, 2)), dma((8, 2)), dma((8, 2)), dma((8, 2)), dma((2,)), dma((2,)),
            dma((chips, 2)), dma((chips, 2)), dma((6, RING)), dma((6, RING)), dma((2, 3)), dma((2, 3)), dma((2,)), dma((2,)),
        ],
        name="block",
        compiler_params=pltpu.CompilerParams(
            collective_id=1, has_side_effects=True, vmem_limit_bytes=62 << 20
        ),
    )(tokens.T, gain, up_weight, down_weight).T


def solution(mesh):
    in_specs = (
        P("tok", ("con", "out")),
        P(("con", "out")),
        P("con", None, "out"),
        P(("con", "out"), None),
    )
    out_specs = P("tok", ("con", "out"))
    return jax.shard_map(local, mesh=mesh, in_specs=in_specs, out_specs=out_specs, check_vma=False)
```
